32 devices in a mesh: grp: 2 (over x), chan: 16 (over z, y, core).
Axes of the slice: x: 2, y: 2, z: 4, core: 2. Of those that a mesh axis runs over, the one named last changes fastest.
Arguments:
- spectra: bfloat16 [128, 4, 2, 4096], P(('grp', 'chan')), parts along dimension 0, may hold values from -60 to 60
- valid: int32 [128, 4], P(('grp', 'chan')), parts along dimension 0, may hold values 0 or 1
- partner: int32 [16], replicated, may hold values from 0 to 15, as said below
- pair_bin: int32 [1024], P(('grp', 'chan')), parts along dimension 0, may hold values from -1 to 127, as said below
- pair_count: int32 [32], P(('grp', 'chan')), parts along dimension 0, may hold values from 24 to 32
Outputs:
- stacked: float32 [256, 1024], P(('grp', 'chan')), parts along dimension 0
The draws below stay inside these ranges and needn't reach their ends.
There are 2 independent parts, one for each index of `grp`. The reference program is written for one: setup_inputs(seed, part) draws one part's arguments, and reference() takes and returns one part's arrays. A program takes and returns all parts, laid end to end along the dimension named above; an argument that names none is the same for every part. Nothing has to cross between parts.
Inputs may be any that keep to these rules, and one draw needn't show every extreme that they name: partner[p] = p XOR r for one r of 1 to 15, the same for every p. `pair_bin`: -1 marks a row without bin, and every row pairing a channel with itself is -1; bin k is owned by block k // 8.
All inputs are finite; a program needn't handle non-finite values. No bound on the sum of `valid` on one device may be relied on, other than what follows from the above.
Results may differ from the reference program's by a relative error of at most 0.0056.
Values may be sent and summed in bfloat16 or wider, within the bound.
A program may use at most 128 MiB of HBM per device.

```python
import math
import jax
import jax.numpy as jnp
from jax import lax

CH_DEV = 4
WIN = 4
F = 4096
BAND = 128
LAGS = 1024
BINS_DEV = 8
PAIRS_DEV = 32
CHANNELS = 64
BINS = 128
N_CHAN = 16


def draw_spectra(key, part):
    nchan = CH_DEV * N_CHAN
    key_base, key_level = jax.random.split(key)
    shape = (nchan, WIN, 2, F // BAND, BAND)
    base = jnp.clip(jax.random.normal(key_base, shape, jnp.float32), -6.0, 6.0)
    levels = jax.random.uniform(key_level, (nchan, WIN, 1, F // BAND, 1), jnp.float32, 0.0, math.log(10.0))
    values = base * jnp.exp(levels)
    return values.reshape(nchan, WIN, 2, F).astype(jnp.bfloat16)


def draw_partner(key, part):
    offset = jax.random.randint(key, (), 1, N_CHAN, dtype=jnp.int32)
    return jnp.bitwise_xor(jnp.arange(N_CHAN, dtype=jnp.int32), offset)


def draw_pair_bin(key, part):
    total = PAIRS_DEV * N_CHAN
    index = jnp.arange(total, dtype=jnp.int32)
    block = index // PAIRS_DEV
    within = index % PAIRS_DEV
    square = CH_DEV * CH_DEV
    first = within % square // CH_DEV
    second = within % CH_DEV
    itself = (within < square) & (first == second)
    key_reach, key_slot = jax.random.split(key)
    distance = jax.random.randint(key_reach, (total,), 0, N_CHAN, dtype=jnp.int32)
    distance = jnp.where(within == 1, N_CHAN - 1, distance)
    distance = jnp.where(within == 2, N_CHAN // 2, distance)
    slot = jax.random.randint(key_slot, (total,), 0, BINS_DEV, dtype=jnp.int32)
    bins = (block + distance) % N_CHAN * BINS_DEV + slot
    return jnp.where(itself, -1, bins).astype(jnp.int32)


def draw_pair_count(key, part):
    lowest = PAIRS_DEV * 3 // 4
    key_count, key_high, key_step = jax.random.split(key, 3)
    counts = jax.random.randint(key_count, (N_CHAN,), lowest, PAIRS_DEV + 1, dtype=jnp.int32)
    high_at = jax.random.randint(key_high, (), 0, N_CHAN, dtype=jnp.int32)
    low_at = (high_at + jax.random.randint(key_step, (), 1, N_CHAN, dtype=jnp.int32)) % N_CHAN
    index = jnp.arange(N_CHAN, dtype=jnp.int32)
    counts = jnp.where(index == high_at, PAIRS_DEV, counts)
    counts = jnp.where(index == low_at, lowest, counts)
    return counts.astype(jnp.int32)


def set_ends(result, key, smallest, largest):
    dims = result.shape
    spot = [jax.random.randint(jax.random.fold_in(key, axis), (), 0, dims[axis]) for axis in range(len(dims))]
    result = result.at[tuple(spot)].set(smallest)
    longest = dims.index(max(dims))
    spot[longest] = (spot[longest] + 1) % dims[longest]
    return result.at[tuple(spot)].set(largest)


def setup_inputs(seed: int = 0, part: int = 0) -> dict:
    seeds = jax.random.split(jax.random.key(seed), 6)
    part_splits = jax.random.split(jax.random.fold_in(seeds[5], part), 6)
    return {
        "spectra": draw_spectra(jax.random.fold_in(jax.random.fold_in(seeds[5], part), 71), part),
        "valid": set_ends((jax.random.randint(part_splits[1], (CHANNELS, WIN), 0, 4) < 3).astype(jnp.int32), jax.random.fold_in(part_splits[1], 1), 0, 1),
        "partner": draw_partner(jax.random.fold_in(seeds[5], 71), part),
        "pair_bin": draw_pair_bin(jax.random.fold_in(jax.random.fold_in(seeds[5], part), 71), part),
        "pair_count": draw_pair_count(jax.random.fold_in(jax.random.fold_in(seeds[5], part), 71), part),
    }


def whiten(spectra, valid):
    values = spectra.astype(jnp.float32)
    power = values[:, :, 0] * values[:, :, 0] + values[:, :, 1] * values[:, :, 1]
    nchan, nwin, nfreq = power.shape
    banded = lax.optimization_barrier(jnp.mean(power.reshape(nchan, nwin, nfreq // BAND, BAND), axis=-1))
    amplitude = jnp.repeat(jnp.sqrt(banded + 1e-06), BAND, axis=-1)
    weights = valid.astype(jnp.float32)[:, :, None, None]
    return (values * weights / amplitude[:, :, None, :]).astype(jnp.bfloat16)

def lag_table():
    freqs = jnp.arange(F, dtype=jnp.int32)
    shifts = jnp.arange(LAGS, dtype=jnp.int32) - LAGS // 2
    phase = jnp.mod(freqs[:, None] * shifts[None, :], 2 * F)
    angle = phase.astype(jnp.float32) * (2.0 * math.pi / (2 * F))
    scale = 1.0 / math.sqrt(F)
    return jnp.concatenate([jnp.cos(angle) * scale, -jnp.sin(angle) * scale], axis=0).astype(jnp.bfloat16)

def correlate(own_block, other_block, table):
    own_real = own_block[:, :, 0].astype(jnp.float32)
    own_imag = own_block[:, :, 1].astype(jnp.float32)
    oth_real = other_block[:, :, 0].astype(jnp.float32)
    oth_imag = other_block[:, :, 1].astype(jnp.float32)
    real_part = jnp.einsum('awf,bwf->abf', own_real, oth_real) + jnp.einsum('awf,bwf->abf', own_imag, oth_imag)
    imag_part = jnp.einsum('awf,bwf->abf', own_imag, oth_real) - jnp.einsum('awf,bwf->abf', own_real, oth_imag)
    nchan = own_block.shape[0]
    nwin = own_block.shape[1]
    spec = (jnp.concatenate([real_part, imag_part], axis=-1) * (1.0 / nwin)).reshape(nchan * nchan, -1)
    spec = spec.astype(jnp.bfloat16)
    return jnp.dot(spec, table, preferred_element_type=jnp.float32)

def reference(spectra, valid, partner, pair_bin, pair_count):
    white = whiten(spectra, valid)
    blocks = white.reshape(N_CHAN, CH_DEV, WIN, 2, F)
    table = lag_table()

    def one_block(block_index):
        own_block = lax.dynamic_index_in_dim(blocks, block_index, 0, keepdims=False)
        other_index = lax.dynamic_index_in_dim(partner, block_index, 0, keepdims=False)
        other_block = lax.dynamic_index_in_dim(blocks, other_index, 0, keepdims=False)
        return jnp.concatenate([correlate(own_block, own_block, table), correlate(own_block, other_block, table)], axis=0)
    corr_all = lax.map(one_block, jnp.arange(N_CHAN, dtype=jnp.int32))
    bins = pair_bin.reshape(N_CHAN, PAIRS_DEV)
    rows = jnp.arange(PAIRS_DEV, dtype=jnp.int32)
    keep = (rows[None, :] < pair_count[:, None]) & (bins >= 0)
    segment = jnp.where(keep, bins, BINS).reshape(-1)
    summed = jax.ops.segment_sum(corr_all.reshape(-1, LAGS), segment, num_segments=BINS + 1)[:BINS]
    return summed * (1.0 / math.sqrt(PAIRS_DEV // BINS_DEV))
```

```python
import functools
import math

import jax
import jax.numpy as jnp
import ml_dtypes
import numpy as np
from jax import lax
from jax.experimental import pallas as pl
from jax.experimental.pallas import tpu as pltpu
from jax.sharding import PartitionSpec as P

F = 4096
BAND = 128
LAGS = 1024
BINS_DEV = 8
PAIRS_DEV = 32
LANES = 128
GROUP = 4


def from_partner(block, axis, bit):
    count = lax.axis_size(axis)
    route = []
    for low in range(count):
        high = low | 1 << bit
        if high != low and high < count:
            route += [(low, high), (high, low)]
    return lax.ppermute(block, axis, route)


def whiten(spectra, valid):
    values = spectra.astype(jnp.float32)
    power = values[:, :, 0] * values[:, :, 0] + values[:, :, 1] * values[:, :, 1]
    nchan, nwin, nfreq = power.shape
    banded = jnp.mean(power.reshape(nchan, nwin, nfreq // BAND, BAND), axis=-1)
    amplitude = jnp.repeat(jnp.sqrt(banded + 1e-06), BAND, axis=-1)
    weights = valid.astype(jnp.float32)[:, :, None, None]
    return (values * weights / amplitude[:, :, None, :]).astype(jnp.bfloat16)


def lag_table():
    freqs = jnp.arange(F, dtype=jnp.int32)
    shifts = jnp.arange(LAGS, dtype=jnp.int32) - LAGS // 2
    phase = jnp.mod(freqs[:, None] * shifts[None, :], 2 * F)
    angle = phase.astype(jnp.float32) * (2.0 * math.pi / (2 * F))
    scale = 1.0 / math.sqrt(F)
    return jnp.concatenate([jnp.cos(angle) * scale, -jnp.sin(angle) * scale], axis=0).astype(
        jnp.bfloat16
    )


def cross_product(left_part, right_part):
    return jnp.einsum("awf,bwf->abf", left_part, right_part, preferred_element_type=jnp.float32)


def correlate(own_block, other_block, table):
    own_real = own_block[:, :, 0]
    own_imag = own_block[:, :, 1]
    oth_real = other_block[:, :, 0]
    oth_imag = other_block[:, :, 1]
    real_part = cross_product(own_real, oth_real) + cross_product(own_imag, oth_imag)
    imag_part = cross_product(own_imag, oth_real) - cross_product(own_real, oth_imag)
    nchan = own_block.shape[0]
    nwin = own_block.shape[1]
    spec = (jnp.concatenate([real_part, imag_part], axis=-1) * (1.0 / nwin)).reshape(
        nchan * nchan, -1
    )
    spec = spec.astype(jnp.bfloat16)
    return jnp.dot(spec, table, preferred_element_type=jnp.float32)


def select_sum(selector, corr_high, corr_low):
    return jnp.dot(selector, corr_high, preferred_element_type=jnp.float32) + jnp.dot(
        selector, corr_low, preferred_element_type=jnp.float32
    )


def on_device_blocks(spectra, valid, partner, pair_bin, pair_count):
    white = whiten(spectra, valid)
    nblocks = lax.axis_size("chan")
    round_mask = partner[0]
    paired = white
    for bit_index in range(nblocks.bit_length() - 1):
        swapped = from_partner(paired, "chan", bit_index)
        paired = jnp.where(round_mask >> bit_index & 1 == 1, swapped, paired)
    table = lag_table()
    self_corr = correlate(white, white, table)
    cross_corr = correlate(white, paired, table)
    corr = jnp.concatenate([self_corr, cross_corr], axis=0)
    corr_high = corr.astype(jnp.bfloat16)
    corr_low = (corr - corr_high.astype(jnp.float32)).astype(jnp.bfloat16)
    rows = jnp.arange(corr.shape[0], dtype=jnp.int32)
    live_rows = (rows < pair_count[0]) & (pair_bin >= 0)
    kept_bins = jnp.where(live_rows, pair_bin, -1)
    targets = lax.iota(jnp.int32, nblocks * BINS_DEV)
    selector = (kept_bins[None, :] == targets[:, None]).astype(jnp.bfloat16)
    terms = select_sum(selector, corr_high, corr_low).reshape(nblocks, BINS_DEV, -1)
    received = lax.all_to_all(terms, "chan", split_axis=0, concat_axis=0, tiled=True)
    summed = jnp.sum(received, axis=0)
    return summed * (1.0 / math.sqrt(PAIRS_DEV // BINS_DEV))


def base_table(nfreq):
    shifts = np.arange(LAGS) - LAGS // 2
    angle = np.mod(np.arange(nfreq)[:, None] * shifts[None, :], 2 * F) * (2.0 * math.pi / (2 * F))
    cos, sin = np.cos(angle), np.sin(angle)
    return np.concatenate(
        [np.concatenate([cos, sin], axis=1), np.concatenate([-sin, cos], axis=1)], axis=0
    ).astype(ml_dtypes.bfloat16)


def slice_phases(nslices, nfreq, scale):
    shifts = np.arange(LAGS) - LAGS // 2
    first = np.arange(nslices) * nfreq
    angle = np.mod(first[:, None] * shifts[None, :], 2 * F) * (2.0 * math.pi / (2 * F))
    both = np.concatenate([np.cos(angle), -np.sin(angle)], axis=1) * scale
    return both.astype(np.float32)[:, None, :]


def expanders(nchan, nwin):
    row = np.arange(LANES)
    per_chan = 2 * nwin
    step = row // (nchan * per_chan)
    first = row // per_chan % nchan
    window = row // 2 % nwin
    second = (first + step) % nchan
    nvalid = nchan * nwin
    pair = first * nchan + second
    lanes = (
        nvalid + pair,
        nvalid + nchan * nchan + pair,
        first * nwin + window,
        second * nwin + window,
    )
    return np.concatenate(
        [(np.arange(LANES)[:, None] == lane[None, :]) for lane in lanes], axis=1
    ).astype(ml_dtypes.bfloat16)


def swap_pairs(rows):
    size = rows.shape[-2]
    axis = rows.ndim - 2
    even = lax.broadcasted_iota(jnp.int32, rows.shape, axis) % 2 == 0
    return jnp.where(
        even, pltpu.roll(rows, size - 1, axis), pltpu.roll(rows, 1, axis)
    ), even


def kernel(
    dims,
    spectra_ref,
    valid_hbm,
    partner_hbm,
    bin_hbm,
    count_hbm,
    expand_hbm,
    table_hbm,
    phase_hbm,
    out_ref,
    valid_ref,
    partner_ref,
    bin_ref,
    count_ref,
    expand_ref,
    meta_ref,
    raw,
    metas,
    table,
    phases,
    rolled,
    turned,
    kept,
    other_valid,
    selector,
    products,
    self_selector,
    spread_selector,
    self_products,
    totals,
    outgoing,
    incoming,
    local_sems,
    send_a,
    recv_a,
    send_m,
    recv_m,
    send_b,
    recv_b,
):
    n, nchan, nwin, nfreq, nbins_dev = dims
    nrow = nchan * nwin * 2
    nbins = n * nbins_dev
    me = lax.axis_index("chan")
    copy_table = pltpu.make_async_copy(table_hbm, table, local_sems.at[0])
    copy_phase = pltpu.make_async_copy(phase_hbm, phases, local_sems.at[1])

    def mine(target):
        return pl.ds(pl.multiple_of(target * nfreq, nfreq), nfreq)

    own_raw = pltpu.make_async_copy(
        spectra_ref.at[:, :, :, mine(me)], raw.at[me], local_sems.at[2]
    )
    own_meta = pltpu.make_async_copy(meta_ref, metas.at[me], local_sems.at[3])
    small = [
        pltpu.make_async_copy(src, dst, local_sems.at[5 + i])
        for i, (src, dst) in enumerate(
            (
                (valid_hbm, valid_ref),
                (bin_hbm, bin_ref),
                (count_hbm, count_ref),
                (partner_hbm, partner_ref),
                (expand_hbm, expand_ref),
            )
        )
    ]
    for copy in small:
        copy.start()

    def peer(k):
        bits = range((n - 1).bit_length())
        return sum((me // 2**b + k // 2**b) % 2 * 2**b for b in bits)

    barrier = pltpu.get_barrier_semaphore()
    for k in range(1, n):
        pl.semaphore_signal(
            barrier,
            inc=1,
            device_id={"chan": peer(k)},
            device_id_type=pl.DeviceIdType.MESH,
        )
    own_raw.start()
    copy_table.start()
    copy_phase.start()
    for copy in small:
        copy.wait()
    lane = lax.broadcasted_iota(jnp.int32, metas.shape[1:], 1)
    meta = jnp.full(metas.shape[1:], count_ref[0], jnp.int32)
    for c in range(nchan):
        for w in range(nwin):
            meta = jnp.where(lane == c * nwin + w, valid_ref[c, w], meta)
    for row in range(2 * nchan * nchan):
        meta = jnp.where(lane == nchan * nwin + row, bin_ref[row], meta)
    meta_ref[...] = meta
    pl.semaphore_wait(barrier, n - 1)
    own_meta.start()

    def remote(src, dst, send, recv, target):
        return pltpu.make_async_remote_copy(
            src_ref=src,
            dst_ref=dst,
            send_sem=send,
            recv_sem=recv,
            device_id={"chan": target},
            device_id_type=pl.DeviceIdType.MESH,
        )

    def meta_copy(k, source):
        return remote(
            meta_ref, metas.at[source], send_m, recv_m, peer(k)
        )

    def raw_copy(k, source):
        target = peer(k)
        return remote(
            spectra_ref.at[:, :, :, mine(target)], raw.at[source], send_a, recv_a.at[group_of[k]], target
        )

    def span(buffer, count, send, recv):
        part = buffer.at[pl.ds(0, count)]
        return remote(part, part, send, recv, peer(1))

    order = range(n - 1, 0, -1)
    arrival = list(range(n // 2)) + list(range(n - 1, n // 2 - 1, -1))
    group_of = {k: i // GROUP for i, k in enumerate(arrival)}
    for k in order:
        meta_copy(k, me).start()
    for k in order:
        raw_copy(k, me).start()

    own_meta.wait()
    span(metas, n - 1, send_m, recv_m).wait_recv()
    values = metas[:, 0, :]
    lane = lax.broadcasted_iota(jnp.int32, (n, LANES), 1)
    nvalid = nchan * nwin
    npairs = 2 * nchan * nchan
    is_count = lane == nvalid + npairs
    count = jnp.sum(jnp.where(is_count, values, 0), axis=1, keepdims=True)
    is_pair = (lane >= nvalid) & (lane < nvalid + npairs)
    dropped = is_pair & ((lane - nvalid >= count) | (values < 0))
    values = jnp.where(dropped, -1, jnp.where(is_count, 0, values))
    spread = jnp.dot(
        values.astype(jnp.float32).astype(jnp.bfloat16),
        expand_ref[...],
        preferred_element_type=jnp.float32,
    )
    self_bin = spread[:, :LANES]
    cross_bin = spread[:, LANES : 2 * LANES]
    first_ok = spread[:, 2 * LANES : 3 * LANES] > 0.5
    second_valid = spread[:, 3 * LANES :]
    self_bin = jnp.where(first_ok & (second_valid > 0.5), self_bin, -1.0)
    cross_bin = jnp.where(first_ok, cross_bin, -1.0)
    for p in range(n):
        kept[p, 0:1, :] = self_bin[p : p + 1]
        kept[p, 1:2, :] = cross_bin[p : p + 1]
        other_valid[p, 0:1, :] = second_valid[p : p + 1]

    bin_rows = lax.broadcasted_iota(jnp.int32, (nbins, LANES), 0).astype(jnp.float32)

    def select(p, carry):
        other = other_valid[partner_ref[p], 0:1, :]
        crossing = jnp.where(other > 0.5, kept[p, 1:2, :], -1.0)
        at = pl.multiple_of(p * LANES, LANES)
        own = kept[p, 0:1, :]
        self_selector[p] = jnp.where(bin_rows == own, 1.0, 0.0).astype(jnp.bfloat16)
        selector[:, pl.ds(at, LANES)] = jnp.where(bin_rows == crossing, 1.0, 0.0).astype(
            jnp.bfloat16
        )
        return carry

    lax.fori_loop(0, n, select, 0)

    def prepare(p):
        x = raw[p].astype(jnp.float32).reshape(nchan, 2 * nwin, nfreq)
        swapped, even = swap_pairs(x)
        power = x * x + swapped * swapped
        scales = []
        for b in range(nfreq // BAND):
            total = jnp.sum(power[:, :, b * BAND : (b + 1) * BAND], axis=-1, keepdims=True)
            scale = lax.rsqrt(total * (1.0 / BAND) + 1e-06)
            scales.append(jnp.broadcast_to(scale, (nchan, 2 * nwin, BAND)))
        scale = jnp.concatenate(scales, axis=-1)
        white = x * scale
        turn = jnp.where(even, -swapped, swapped) * scale
        for s in range(nchan):
            at = s * nrow
            part = jnp.concatenate([white[s:], white[:s]], axis=0) if s else white
            rolled[p, at : at + nrow, :] = part.reshape(nrow, nfreq).astype(jnp.bfloat16)
            part = jnp.concatenate([turn[s:], turn[:s]], axis=0) if s else turn
            turned[p, at : at + nrow, :] = part.reshape(nrow, nfreq).astype(jnp.bfloat16)

    def multiply_self(p, slot):
        x = rolled[p, 0:nrow, :]
        for s in range(nchan):
            here = slice(s * nrow, (s + 1) * nrow)
            rows = slice(slot * LANES + s * nrow, slot * LANES + (s + 1) * nrow)
            self_products[rows, 0:nfreq] = x * rolled[p, here, :]
            self_products[rows, nfreq : 2 * nfreq] = x * turned[p, here, :]

    totals[...] = jnp.zeros_like(totals)

    def add_group(members):
        for slot, p in enumerate(members):
            multiply_self(p, slot)
            spread_selector[:, slot * LANES : (slot + 1) * LANES] = self_selector[p]
        totals[...] += jnp.dot(
            spread_selector[...], self_products[...], preferred_element_type=jnp.float32
        )

    for g in range(0, n, GROUP):
        ks = arrival[g : g + GROUP]
        members = [peer(k) for k in ks]
        if 0 in ks:
            own_raw.wait()
        remote_count = sum(k != 0 for k in ks)
        if remote_count:
            span(raw, remote_count, send_a, recv_a.at[g // GROUP]).wait_recv()
        for source in members:
            prepare(source)
        add_group(members)

    def multiply(p):
        q = partner_ref[p]
        x = rolled[p, 0:nrow, :]
        at = pl.multiple_of(p * LANES, LANES)
        for s in range(nchan):
            here = slice(s * nrow, (s + 1) * nrow)
            mid = at + s * nrow
            products[pl.ds(mid, nrow), 0:nfreq] = x * rolled[q, here, :]
            products[pl.ds(mid, nrow), nfreq : 2 * nfreq] = x * turned[q, here, :]

    def multiply_four(i, carry):
        for j in range(4):
            multiply(4 * i + j)
        return carry

    lax.fori_loop(0, n // 4, multiply_four, 0)

    terms = totals[...] + jnp.dot(
        selector[...], products[...], preferred_element_type=jnp.float32
    )
    outgoing[...] = terms.reshape(n, nbins_dev, 2 * nfreq).astype(jnp.bfloat16)

    def term_copy(k, source):
        target = peer(k)
        return remote(
            outgoing.at[target], incoming.at[source], send_b, recv_b, target
        )

    own_terms = pltpu.make_async_copy(outgoing.at[me], incoming.at[me], local_sems.at[4])
    for k in order:
        term_copy(k, me).start()
    own_terms.start()
    copy_table.wait()
    copy_phase.wait()
    own_terms.wait()
    span(incoming, n - 1, send_b, recv_b).wait_recv()

    stacked = incoming[...].astype(jnp.float32).reshape(nbins, 2 * nfreq).astype(jnp.bfloat16)
    lags = jnp.dot(stacked, table[...], preferred_element_type=jnp.float32)
    lags = jnp.sum(lags.reshape(n, nbins_dev, 2 * LAGS) * phases[...], axis=0)
    out_ref[...] = lags[:, :LAGS] + lags[:, LAGS:]

    span(metas, n - 1, send_m, recv_m).wait_send()
    span(raw, n - 1, send_a, recv_a.at[0]).wait_send()
    span(incoming, n - 1, send_b, recv_b).wait_send()


def on_device_slices(spectra, valid, partner, pair_bin, pair_count):
    n = lax.axis_size("chan")
    nchan, nwin, _, nfreq_all = spectra.shape
    nfreq = nfreq_all // n
    nrow = nchan * nwin * 2
    nbins = n * BINS_DEV
    scale = 1.0 / (math.sqrt(nfreq_all) * nwin * math.sqrt(PAIRS_DEV // BINS_DEV))
    hbm = pl.BlockSpec(memory_space=pltpu.HBM)
    vmem = pl.BlockSpec(memory_space=pltpu.VMEM)
    dma = pltpu.SemaphoreType.DMA
    return pl.pallas_call(
        functools.partial(kernel, (n, nchan, nwin, nfreq, BINS_DEV)),
        out_shape=pltpu.VMEM((BINS_DEV, LAGS), jnp.float32),
        in_specs=[hbm] * 8,
        out_specs=vmem,
        scratch_shapes=[
            pltpu.SMEM(valid.shape, jnp.int32),
            pltpu.SMEM(partner.shape, jnp.int32),
            pltpu.SMEM(pair_bin.shape, jnp.int32),
            pltpu.SMEM(pair_count.shape, jnp.int32),
            pltpu.VMEM((LANES, 4 * LANES), jnp.bfloat16),
            pltpu.VMEM((1, LANES), jnp.int32),
            pltpu.VMEM((n, nchan, nwin, 2, nfreq), jnp.bfloat16),
            pltpu.VMEM((n, 1, LANES), jnp.int32),
            pltpu.VMEM((2 * nfreq, 2 * LAGS), jnp.bfloat16),
            pltpu.VMEM((n, 1, 2 * LAGS), jnp.float32),
            pltpu.VMEM((n, nchan * nrow, nfreq), jnp.bfloat16),
            pltpu.VMEM((n, nchan * nrow, nfreq), jnp.bfloat16),
            pltpu.VMEM((n, 8, LANES), jnp.float32),
            pltpu.VMEM((n, 8, LANES), jnp.float32),
            pltpu.VMEM((nbins, n * LANES), jnp.bfloat16),
            pltpu.VMEM((n * LANES, 2 * nfreq), jnp.bfloat16),
            pltpu.VMEM((n, nbins, LANES), jnp.bfloat16),
            pltpu.VMEM((nbins, GROUP * LANES), jnp.bfloat16),
            pltpu.VMEM((GROUP * LANES, 2 * nfreq), jnp.bfloat16),
            pltpu.VMEM((nbins, 2 * nfreq), jnp.float32),
            pltpu.VMEM((n, BINS_DEV, 2 * nfreq), jnp.bfloat16),
            pltpu.VMEM((n, BINS_DEV, 2 * nfreq), jnp.bfloat16),
            dma((10,)),
            dma,
            dma((n // GROUP,)),
            dma,
            dma,
            dma,
            dma,
        ],
        compiler_params=pltpu.CompilerParams(
            collective_id=0, has_side_effects=True, vmem_limit_bytes=60 * 1024 * 1024
        ),
    )(
        spectra,
        valid,
        partner,
        pair_bin,
        pair_count,
        jnp.asarray(expanders(nchan, nwin)),
        jnp.asarray(base_table(nfreq)),
        jnp.asarray(slice_phases(n, nfreq, scale)),
    )


def solution(mesh):
    in_specs = (
        P(("grp", "chan"), None, None, None),
        P(("grp", "chan"), None),
        P(),
        P(("grp", "chan")),
        P(("grp", "chan")),
    )
    out_specs = P(("grp", "chan"), None)
    whole_bands = F % (mesh.shape["chan"] * BAND) == 0
    return jax.shard_map(
        on_device_slices if whole_bands else on_device_blocks,
        mesh=mesh,
        in_specs=in_specs,
        out_specs=out_specs,
        check_vma=False,
    )
```

```python
import functools
import math

import jax
import jax.numpy as jnp
import ml_dtypes
import numpy as np
from jax import lax
from jax.experimental import pallas as pl
from jax.experimental.pallas import tpu as pltpu
from jax.sharding import PartitionSpec as P

F = 4096
BAND = 128
LAGS = 1024
BINS_DEV = 8
PAIRS_DEV = 32
LANES = 128
GROUP = 4
PLANE = 4


def from_partner(block, axis, bit):
    count = lax.axis_size(axis)
    route = []
    for low in range(count):
        high = low | 1 << bit
        if high != low and high < count:
            route += [(low, high), (high, low)]
    return lax.ppermute(block, axis, route)


def whiten(spectra, valid):
    values = spectra.astype(jnp.float32)
    power = values[:, :, 0] * values[:, :, 0] + values[:, :, 1] * values[:, :, 1]
    nchan, nwin, nfreq = power.shape
    banded = jnp.mean(power.reshape(nchan, nwin, nfreq // BAND, BAND), axis=-1)
    amplitude = jnp.repeat(jnp.sqrt(banded + 1e-06), BAND, axis=-1)
    weights = valid.astype(jnp.float32)[:, :, None, None]
    return (values * weights / amplitude[:, :, None, :]).astype(jnp.bfloat16)


def lag_table():
    freqs = jnp.arange(F, dtype=jnp.int32)
    shifts = jnp.arange(LAGS, dtype=jnp.int32) - LAGS // 2
    phase = jnp.mod(freqs[:, None] * shifts[None, :], 2 * F)
    angle = phase.astype(jnp.float32) * (2.0 * math.pi / (2 * F))
    scale = 1.0 / math.sqrt(F)
    return jnp.concatenate([jnp.cos(angle) * scale, -jnp.sin(angle) * scale], axis=0).astype(
        jnp.bfloat16
    )


def cross_product(left_part, right_part):
    return jnp.einsum("awf,bwf->abf", left_part, right_part, preferred_element_type=jnp.float32)


def correlate(own_block, other_block, table):
    own_real = own_block[:, :, 0]
    own_imag = own_block[:, :, 1]
    oth_real = other_block[:, :, 0]
    oth_imag = other_block[:, :, 1]
    real_part = cross_product(own_real, oth_real) + cross_product(own_imag, oth_imag)
    imag_part = cross_product(own_imag, oth_real) - cross_product(own_real, oth_imag)
    nchan = own_block.shape[0]
    nwin = own_block.shape[1]
    spec = (jnp.concatenate([real_part, imag_part], axis=-1) * (1.0 / nwin)).reshape(
        nchan * nchan, -1
    )
    spec = spec.astype(jnp.bfloat16)
    return jnp.dot(spec, table, preferred_element_type=jnp.float32)


def select_sum(selector, corr_high, corr_low):
    return jnp.dot(selector, corr_high, preferred_element_type=jnp.float32) + jnp.dot(
        selector, corr_low, preferred_element_type=jnp.float32
    )


def on_device_blocks(spectra, valid, partner, pair_bin, pair_count):
    white = whiten(spectra, valid)
    nblocks = lax.axis_size("chan")
    round_mask = partner[0]
    paired = white
    for bit_index in range(nblocks.bit_length() - 1):
        swapped = from_partner(paired, "chan", bit_index)
        paired = jnp.where(round_mask >> bit_index & 1 == 1, swapped, paired)
    table = lag_table()
    self_corr = correlate(white, white, table)
    cross_corr = correlate(white, paired, table)
    corr = jnp.concatenate([self_corr, cross_corr], axis=0)
    corr_high = corr.astype(jnp.bfloat16)
    corr_low = (corr - corr_high.astype(jnp.float32)).astype(jnp.bfloat16)
    rows = jnp.arange(corr.shape[0], dtype=jnp.int32)
    live_rows = (rows < pair_count[0]) & (pair_bin >= 0)
    kept_bins = jnp.where(live_rows, pair_bin, -1)
    targets = lax.iota(jnp.int32, nblocks * BINS_DEV)
    selector = (kept_bins[None, :] == targets[:, None]).astype(jnp.bfloat16)
    terms = select_sum(selector, corr_high, corr_low).reshape(nblocks, BINS_DEV, -1)
    received = lax.all_to_all(terms, "chan", split_axis=0, concat_axis=0, tiled=True)
    summed = jnp.sum(received, axis=0)
    return summed * (1.0 / math.sqrt(PAIRS_DEV // BINS_DEV))


def base_table(nfreq):
    shifts = np.arange(LAGS) - LAGS // 2
    angle = np.mod(np.arange(nfreq)[:, None] * shifts[None, :], 2 * F) * (2.0 * math.pi / (2 * F))
    cos, sin = np.cos(angle), np.sin(angle)
    return np.concatenate(
        [np.concatenate([cos, sin], axis=1), np.concatenate([-sin, cos], axis=1)], axis=0
    ).astype(ml_dtypes.bfloat16)


def slice_phases(nslices, nfreq, scale):
    shifts = np.arange(LAGS) - LAGS // 2
    first = np.arange(nslices) * nfreq
    angle = np.mod(first[:, None] * shifts[None, :], 2 * F) * (2.0 * math.pi / (2 * F))
    both = np.concatenate([np.cos(angle), -np.sin(angle)], axis=1) * scale
    return both.astype(np.float32)[:, None, :]


def expanders(nchan, nwin):
    row = np.arange(LANES)
    per_chan = 2 * nwin
    chan = row // per_chan % nchan
    shift = row // (per_chan * nchan)
    npairs = nchan * nchan

    def pair(step):
        return chan * nchan + (chan + step) % nchan

    def reverse(step):
        return (chan + step) % nchan * nchan + chan

    lanes = (
        pair(0),
        pair(1),
        reverse(1),
        pair(2),
        npairs + pair(shift),
        npairs + reverse(shift),
    )
    return np.concatenate(
        [(np.arange(LANES)[:, None] == lane[None, :]) for lane in lanes], axis=1
    ).astype(ml_dtypes.bfloat16)


def swap_pairs(rows):
    size = rows.shape[-2]
    axis = rows.ndim - 2
    even = lax.broadcasted_iota(jnp.int32, rows.shape, axis) % 2 == 0
    return jnp.where(
        even, pltpu.roll(rows, size - 1, axis), pltpu.roll(rows, 1, axis)
    ), even


def halves_swapped(rows):
    half = rows.shape[0] // 2
    return jnp.concatenate([rows[half:], rows[:half]], axis=0)


def kernel(
    dims,
    spectra_hbm,
    valid_hbm,
    partner_hbm,
    bin_hbm,
    count_hbm,
    expand_hbm,
    table_hbm,
    phase_hbm,
    out_ref,
    own,
    valid_ref,
    partner_ref,
    bin_ref,
    count_ref,
    expand_ref,
    meta_ref,
    metas,
    white,
    plain,
    odd,
    plain_turn,
    odd_turn,
    table,
    phases,
    cross_bins,
    select_re,
    select_im,
    last_re,
    last_im,
    products,
    last_products,
    total_re,
    total_im,
    outgoing,
    incoming,
    local_sems,
    send_a,
    recv_a,
    send_m,
    recv_m,
    send_b,
    recv_b,
    ready,
    token,
):
    n, nchan, nwin, nfreq, nbins_dev = dims
    nrow = nchan * nwin * 2
    nbins = n * nbins_dev
    npairs = nchan * nchan
    ngroups = n // GROUP
    me = lax.axis_index("chan")

    def peer(k):
        bits = range((n - 1).bit_length())
        return sum((me // 2**b + k // 2**b) % 2 * 2**b for b in bits)

    def remote(src, dst, send, recv, target):
        return pltpu.make_async_remote_copy(
            src_ref=src,
            dst_ref=dst,
            send_sem=send,
            recv_sem=recv,
            device_id={"chan": target},
            device_id_type=pl.DeviceIdType.MESH,
        )

    def span(buffer, first, count, send, recv):
        part = buffer.at[pl.ds(first, count)]
        return remote(part, part, send, recv, peer(1))

    copy_own = pltpu.make_async_copy(spectra_hbm, own, local_sems.at[0])
    copy_table = pltpu.make_async_copy(table_hbm, table, local_sems.at[1])
    copy_phase = pltpu.make_async_copy(phase_hbm, phases, local_sems.at[2])
    small = [
        pltpu.make_async_copy(src, dst, local_sems.at[3 + i])
        for i, (src, dst) in enumerate(
            (
                (valid_hbm, valid_ref),
                (bin_hbm, bin_ref),
                (count_hbm, count_ref),
                (partner_hbm, partner_ref),
                (expand_hbm, expand_ref),
            )
        )
    ]
    copy_own.start()
    for copy in small[:3]:
        copy.start()
    plane = me // PLANE
    is_last = plane == n // PLANE - 1
    barrier = pltpu.get_barrier_semaphore()

    def signal(sem, ks):
        for k in ks:
            pl.semaphore_signal(
                sem,
                inc=1,
                device_id={"chan": peer(k)},
                device_id_type=pl.DeviceIdType.MESH,
            )

    @pl.when(jnp.logical_not(is_last))
    def _():
        signal(barrier, range(n - 1, 0, -1))

    for copy in small[3:]:
        copy.start()
    copy_table.start()
    copy_phase.start()
    for copy in small[:3]:
        copy.wait()

    lane = lax.broadcasted_iota(jnp.int32, meta_ref.shape, 1)
    bins = jnp.full(meta_ref.shape, -1, jnp.int32)
    for row in range(2 * npairs):
        bins = jnp.where(lane == row, bin_ref[row], bins)
    bins = jnp.where((lane < count_ref[0]) & (bins >= 0), bins, -1)
    meta_ref[...] = bins

    sub = lax.broadcasted_iota(jnp.int32, (nchan, 2 * nwin, LANES), 1) // 2
    chan = lax.broadcasted_iota(jnp.int32, (nchan, 2 * nwin, LANES), 0)
    usable = jnp.zeros((nchan, 2 * nwin, LANES), jnp.float32)
    for c in range(nchan):
        for w in range(nwin):
            usable = jnp.where(
                (chan == c) & (sub == w), valid_ref[c, w].astype(jnp.float32), usable
            )

    def whiten_slice(t):
        here = pl.ds(pl.multiple_of(t * nfreq, nfreq), nfreq)
        x = own[:, :, :, here].astype(jnp.float32)
        x = x.reshape(nchan, 2 * nwin, nfreq)
        swapped, _ = swap_pairs(x)
        power = x * x + swapped * swapped
        for b in range(nfreq // BAND):
            band = slice(b * BAND, (b + 1) * BAND)
            total = jnp.sum(power[:, :, band], axis=-1, keepdims=True)
            scale = lax.rsqrt(total * (1.0 / BAND) + 1e-06) * usable
            rows = (x[:, :, band] * scale).reshape(nrow, BAND)
            white[t, :, band] = rows.astype(jnp.bfloat16)

    def send_meta(k):
        remote(meta_ref, metas.at[k], send_m, recv_m, peer(k)).start()

    def send_white(k):
        remote(white.at[peer(k)], plain.at[k], send_a, recv_a.at[k // GROUP], peer(k)).start()

    def each(act, ks):
        for k in ks:
            act(k)

    near = [7, 6, 5, 4]
    middle = [11, 10, 9, 8]
    far = [15, 14, 13, 12]
    inside = [3, 2, 1]
    copy_own.wait()

    @pl.when(jnp.logical_not(is_last))
    def _():
        def step(i, carry):
            for u in range(4):
                whiten_slice(4 * i + u)
            return carry

        lax.fori_loop(0, n // 4, step, 0)
        pl.semaphore_wait(barrier, 3 * PLANE - 1)

    @pl.when(is_last)
    def _():
        pl.semaphore_wait(barrier, 3 * PLANE)
        signal(ready, far + middle + near)
        each(send_meta, far + middle + near)
        for k in far + middle + near:
            whiten_slice(peer(k))
            send_white(k)
        for k in [*inside, 0]:
            whiten_slice(peer(k))
        pl.semaphore_wait(token, 1)
        each(send_meta, inside)
        each(send_white, inside)

    @pl.when(plane == 2)
    def _():
        each(send_meta, far + middle + inside)
        each(send_white, far + middle)
        pl.semaphore_wait(ready, PLANE)
        signal(token, near[-1:])
        each(send_meta, near)
        each(send_white, near + inside)

    @pl.when(plane == 1)
    def _():
        each(send_meta, far + near + inside)
        each(send_white, far + near)
        pl.semaphore_wait(ready, PLANE)
        each(send_meta, middle)
        each(send_white, middle + inside)

    @pl.when(plane == 0)
    def _():
        each(send_meta, middle + near + inside)
        each(send_white, middle)
        pl.semaphore_wait(ready, PLANE)
        each(send_meta, far)
        each(send_white, far + near + inside)

    order = range(n - 1, 0, -1)

    plain[0] = white[me]
    metas[0] = meta_ref[...]
    for copy in small[3:]:
        copy.wait()
    mirror = partner_ref[0]
    firsts = []
    for j in range(n // 2):
        first = j
        for b in reversed(range((n - 1).bit_length())):
            spread = j // 2**b * 2 ** (b + 1) + j % 2**b
            first = jnp.where((mirror >> b) % 2 == 1, spread, first)
        firsts.append(first)

    def prepare(k):
        x = plain[k].astype(jnp.float32)
        swapped, even = swap_pairs(x)
        turn = jnp.where(even, -swapped, swapped)
        step = 2 * nwin
        odd[k] = jnp.concatenate([x[step:], x[:step]], axis=0).astype(jnp.bfloat16)
        plain_turn[k] = turn.astype(jnp.bfloat16)
        odd_turn[k] = jnp.concatenate([turn[step:], turn[:step]], axis=0).astype(jnp.bfloat16)

    def put(target, at, left, right, right_turn):
        target[pl.ds(at, nrow), 0:nfreq] = left * right
        target[pl.ds(at, nrow), nfreq : 2 * nfreq] = left * right_turn

    def multiply_self(target, g):
        for u in range(GROUP):
            k = g * GROUP + u
            x = plain[k]
            xt = plain_turn[k]
            put(target, u * nrow, x, x, xt)
            put(target, LANES + u * nrow, x, odd[k], odd_turn[k])
            put(target, 2 * LANES + u * nrow, x, halves_swapped(x), halves_swapped(xt))

    span(metas, 1, n - 1, send_m, recv_m).wait_recv()
    spread = jnp.dot(
        metas[:, 0, :].astype(jnp.float32).astype(jnp.bfloat16),
        expand_ref[...],
        preferred_element_type=jnp.float32,
    )
    for k in range(n):
        cross_bins[k, 0:1, :] = spread[k : k + 1, 4 * LANES : 5 * LANES]
        cross_bins[k, 1:2, :] = spread[k : k + 1, 5 * LANES : 6 * LANES]
    self_bins = spread[:, : 4 * LANES]
    slot = lax.broadcasted_iota(jnp.int32, self_bins.shape, 0) % GROUP
    place = lax.broadcasted_iota(jnp.int32, self_bins.shape, 1) % LANES // nrow
    self_bins = jnp.where(slot == place, self_bins, 0.0)
    bin_rows = lax.broadcasted_iota(jnp.int32, (nbins, LANES), 0).astype(jnp.float32)

    def one_hot(row):
        return jnp.where(bin_rows == row, 1.0, 0.0)

    for g in range(ngroups):
        row = jnp.sum(self_bins[g * GROUP : (g + 1) * GROUP], axis=0, keepdims=True)
        same, ahead, back, across = [
            one_hot(row[:, i * LANES : (i + 1) * LANES]) for i in range(4)
        ]
        final = g == ngroups - 1
        for target, middle in (
            (last_re if final else select_re.at[g], ahead + back),
            (last_im if final else select_im.at[g], ahead - back),
        ):
            target[:, 0:LANES] = same.astype(jnp.bfloat16)
            target[:, LANES : 2 * LANES] = middle.astype(jnp.bfloat16)
            target[:, 2 * LANES : 3 * LANES] = across.astype(jnp.bfloat16)
    base = 3 * LANES
    for j in range(n // 2):
        ahead = one_hot(cross_bins[firsts[j], 0:1, :])
        back = one_hot(cross_bins[firsts[j] ^ mirror, 1:2, :])
        here = slice(base + j * LANES, base + (j + 1) * LANES)
        last_re[:, here] = (ahead + back).astype(jnp.bfloat16)
        last_im[:, here] = (ahead - back).astype(jnp.bfloat16)

    def product(left, right):
        return jnp.dot(left, right, preferred_element_type=jnp.float32)

    for g in range(ngroups):
        here = range(max(g * GROUP, 1), (g + 1) * GROUP)
        span(plain, here[0], len(here), send_a, recv_a.at[g]).wait_recv()
        for k in range(g * GROUP, (g + 1) * GROUP):
            prepare(k)
        if g < ngroups - 1:
            multiply_self(products, g)
            part_re = product(select_re[g], products[:, 0:nfreq])
            part_im = product(select_im[g], products[:, nfreq : 2 * nfreq])
            total_re[...] = part_re if g == 0 else total_re[...] + part_re
            total_im[...] = part_im if g == 0 else total_im[...] + part_im
        else:
            multiply_self(last_products, g)

    for j in range(n // 2):
        x = plain[firsts[j]]
        q = firsts[j] ^ mirror
        at = base + j * LANES
        y, yt, z, zt = plain[q], plain_turn[q], odd[q], odd_turn[q]
        put(last_products, at, x, y, yt)
        put(last_products, at + nrow, x, z, zt)
        put(last_products, at + 2 * nrow, x, halves_swapped(y), halves_swapped(yt))
        put(last_products, at + 3 * nrow, x, halves_swapped(z), halves_swapped(zt))

    terms_re = total_re[...] + product(last_re[...], last_products[:, 0:nfreq])
    outgoing[:, :, 0:nfreq] = terms_re.reshape(n, nbins_dev, nfreq).astype(jnp.bfloat16)
    terms_im = total_im[...] + product(last_im[...], last_products[:, nfreq : 2 * nfreq])
    outgoing[:, :, nfreq : 2 * nfreq] = terms_im.reshape(n, nbins_dev, nfreq).astype(jnp.bfloat16)

    for k in order:
        remote(outgoing.at[peer(k)], incoming.at[me], send_b, recv_b, peer(k)).start()
    incoming[me] = outgoing[me]
    copy_table.wait()
    copy_phase.wait()
    span(incoming, 0, n - 1, send_b, recv_b).wait_recv()

    stacked = incoming[...].astype(jnp.float32).reshape(nbins, 2 * nfreq).astype(jnp.bfloat16)
    lags = product(stacked, table[...])
    lags = jnp.sum(lags.reshape(n, nbins_dev, 2 * LAGS) * phases[...], axis=0)
    out_ref[...] = lags[:, :LAGS] + lags[:, LAGS:]

    span(metas, 1, n - 1, send_m, recv_m).wait_send()
    span(plain, 1, n - 1, send_a, recv_a.at[0]).wait_send()
    span(incoming, 0, n - 1, send_b, recv_b).wait_send()


def on_device_slices(spectra, valid, partner, pair_bin, pair_count):
    n = lax.axis_size("chan")
    nchan, nwin, _, nfreq_all = spectra.shape
    nfreq = nfreq_all // n
    nrow = nchan * nwin * 2
    nbins = n * BINS_DEV
    base = 3 * LANES
    deep = base + n // 2 * LANES
    scale = 1.0 / (math.sqrt(nfreq_all) * nwin * math.sqrt(PAIRS_DEV // BINS_DEV))
    hbm = pl.BlockSpec(memory_space=pltpu.HBM)
    vmem = pl.BlockSpec(memory_space=pltpu.VMEM)
    dma = pltpu.SemaphoreType.DMA
    bf16 = jnp.bfloat16
    return pl.pallas_call(
        functools.partial(kernel, (n, nchan, nwin, nfreq, BINS_DEV)),
        out_shape=pltpu.VMEM((BINS_DEV, LAGS), jnp.float32),
        in_specs=[hbm] * 8,
        out_specs=vmem,
        scratch_shapes=[
            pltpu.VMEM(spectra.shape, bf16),
            pltpu.SMEM(valid.shape, jnp.int32),
            pltpu.SMEM(partner.shape, jnp.int32),
            pltpu.SMEM(pair_bin.shape, jnp.int32),
            pltpu.SMEM(pair_count.shape, jnp.int32),
            pltpu.VMEM((LANES, 6 * LANES), bf16),
            pltpu.VMEM((1, LANES), jnp.int32),
            pltpu.VMEM((n, 1, LANES), jnp.int32),
            pltpu.VMEM((n, nrow, nfreq), bf16),
            pltpu.VMEM((n, nrow, nfreq), bf16),
            pltpu.VMEM((n, nrow, nfreq), bf16),
            pltpu.VMEM((n, nrow, nfreq), bf16),
            pltpu.VMEM((n, nrow, nfreq), bf16),
            pltpu.VMEM((2 * nfreq, 2 * LAGS), bf16),
            pltpu.VMEM((n, 1, 2 * LAGS), jnp.float32),
            pltpu.VMEM((n, 8, LANES), jnp.float32),
            pltpu.VMEM((n // GROUP - 1, nbins, base), bf16),
            pltpu.VMEM((n // GROUP - 1, nbins, base), bf16),
            pltpu.VMEM((nbins, deep), bf16),
            pltpu.VMEM((nbins, deep), bf16),
            pltpu.VMEM((base, 2 * nfreq), bf16),
            pltpu.VMEM((deep, 2 * nfreq), bf16),
            pltpu.VMEM((nbins, nfreq), jnp.float32),
            pltpu.VMEM((nbins, nfreq), jnp.float32),
            pltpu.VMEM((n, BINS_DEV, 2 * nfreq), bf16),
            pltpu.VMEM((n, BINS_DEV, 2 * nfreq), bf16),
            dma((8,)),
            dma,
            dma((n // GROUP,)),
            dma,
            dma,
            dma,
            dma,
            pltpu.SemaphoreType.REGULAR,
            pltpu.SemaphoreType.REGULAR,
        ],
        compiler_params=pltpu.CompilerParams(
            collective_id=0, has_side_effects=True, vmem_limit_bytes=60 * 1024 * 1024
        ),
    )(
        spectra,
        valid,
        partner,
        pair_bin,
        pair_count,
        jnp.asarray(expanders(nchan, nwin)),
        jnp.asarray(base_table(nfreq)),
        jnp.asarray(slice_phases(n, nfreq, scale)),
    )


def solution(mesh):
    in_specs = (
        P(("grp", "chan"), None, None, None),
        P(("grp", "chan"), None),
        P(),
        P(("grp", "chan")),
        P(("grp", "chan")),
    )
    out_specs = P(("grp", "chan"), None)
    whole_bands = F % (mesh.shape["chan"] * BAND) == 0
    return jax.shard_map(
        on_device_slices if whole_bands else on_device_blocks,
        mesh=mesh,
        in_specs=in_specs,
        out_specs=out_specs,
        check_vma=False,
    )
```

```python
import functools
import math

import jax
import jax.numpy as jnp
import ml_dtypes
import numpy as np
from jax import lax
from jax.experimental import pallas as pl
from jax.experimental.pallas import tpu as pltpu
from jax.sharding import PartitionSpec as P

F = 4096
BAND = 128
LAGS = 1024
BINS_DEV = 8
PAIRS_DEV = 32
LANES = 128
GROUP = 4
PLANE = 4


def from_partner(block, axis, bit):
    count = lax.axis_size(axis)
    route = []
    for low in range(count):
        high = low | 1 << bit
        if high != low and high < count:
            route += [(low, high), (high, low)]
    return lax.ppermute(block, axis, route)


def whiten(spectra, valid):
    values = spectra.astype(jnp.float32)
    power = values[:, :, 0] * values[:, :, 0] + values[:, :, 1] * values[:, :, 1]
    nchan, nwin, nfreq = power.shape
    banded = jnp.mean(power.reshape(nchan, nwin, nfreq // BAND, BAND), axis=-1)
    amplitude = jnp.repeat(jnp.sqrt(banded + 1e-06), BAND, axis=-1)
    weights = valid.astype(jnp.float32)[:, :, None, None]
    return (values * weights / amplitude[:, :, None, :]).astype(jnp.bfloat16)


def lag_table():
    freqs = jnp.arange(F, dtype=jnp.int32)
    shifts = jnp.arange(LAGS, dtype=jnp.int32) - LAGS // 2
    phase = jnp.mod(freqs[:, None] * shifts[None, :], 2 * F)
    angle = phase.astype(jnp.float32) * (2.0 * math.pi / (2 * F))
    scale = 1.0 / math.sqrt(F)
    return jnp.concatenate([jnp.cos(angle) * scale, -jnp.sin(angle) * scale], axis=0).astype(
        jnp.bfloat16
    )


def cross_product(left_part, right_part):
    return jnp.einsum("awf,bwf->abf", left_part, right_part, preferred_element_type=jnp.float32)


def correlate(own_block, other_block, table):
    own_real = own_block[:, :, 0]
    own_imag = own_block[:, :, 1]
    oth_real = other_block[:, :, 0]
    oth_imag = other_block[:, :, 1]
    real_part = cross_product(own_real, oth_real) + cross_product(own_imag, oth_imag)
    imag_part = cross_product(own_imag, oth_real) - cross_product(own_real, oth_imag)
    nchan = own_block.shape[0]
    nwin = own_block.shape[1]
    spec = (jnp.concatenate([real_part, imag_part], axis=-1) * (1.0 / nwin)).reshape(
        nchan * nchan, -1
    )
    spec = spec.astype(jnp.bfloat16)
    return jnp.dot(spec, table, preferred_element_type=jnp.float32)


def select_sum(selector, corr_high, corr_low):
    return jnp.dot(selector, corr_high, preferred_element_type=jnp.float32) + jnp.dot(
        selector, corr_low, preferred_element_type=jnp.float32
    )


def on_device_blocks(spectra, valid, partner, pair_bin, pair_count):
    white = whiten(spectra, valid)
    nblocks = lax.axis_size("chan")
    round_mask = partner[0]
    paired = white
    for bit_index in range(nblocks.bit_length() - 1):
        swapped = from_partner(paired, "chan", bit_index)
        paired = jnp.where(round_mask >> bit_index & 1 == 1, swapped, paired)
    table = lag_table()
    self_corr = correlate(white, white, table)
    cross_corr = correlate(white, paired, table)
    corr = jnp.concatenate([self_corr, cross_corr], axis=0)
    corr_high = corr.astype(jnp.bfloat16)
    corr_low = (corr - corr_high.astype(jnp.float32)).astype(jnp.bfloat16)
    rows = jnp.arange(corr.shape[0], dtype=jnp.int32)
    live_rows = (rows < pair_count[0]) & (pair_bin >= 0)
    kept_bins = jnp.where(live_rows, pair_bin, -1)
    targets = lax.iota(jnp.int32, nblocks * BINS_DEV)
    selector = (kept_bins[None, :] == targets[:, None]).astype(jnp.bfloat16)
    terms = select_sum(selector, corr_high, corr_low).reshape(nblocks, BINS_DEV, -1)
    received = lax.all_to_all(terms, "chan", split_axis=0, concat_axis=0, tiled=True)
    summed = jnp.sum(received, axis=0)
    return summed * (1.0 / math.sqrt(PAIRS_DEV // BINS_DEV))


def base_table(nfreq):
    shifts = np.arange(LAGS) - LAGS // 2
    angle = np.mod(np.arange(nfreq)[:, None] * shifts[None, :], 2 * F) * (2.0 * math.pi / (2 * F))
    cos, sin = np.cos(angle), np.sin(angle)
    return np.concatenate(
        [np.concatenate([cos, sin], axis=1), np.concatenate([-sin, cos], axis=1)], axis=0
    ).astype(ml_dtypes.bfloat16)


def slice_phases(nslices, nfreq, scale):
    shifts = np.arange(LAGS) - LAGS // 2
    first = np.arange(nslices) * nfreq
    angle = np.mod(first[:, None] * shifts[None, :], 2 * F) * (2.0 * math.pi / (2 * F))
    both = np.concatenate([np.cos(angle), -np.sin(angle)], axis=1) * scale
    return both.astype(np.float32)[:, None, :]


def expanders(nchan, nwin):
    row = np.arange(LANES)
    per_chan = 2 * nwin
    chan = row // per_chan % nchan
    shift = row // (per_chan * nchan)
    npairs = nchan * nchan

    def pair(step):
        return chan * nchan + (chan + step) % nchan

    def reverse(step):
        return (chan + step) % nchan * nchan + chan

    lanes = (
        pair(0),
        pair(1),
        reverse(1),
        pair(2),
        npairs + pair(shift),
        npairs + reverse(shift),
    )
    return np.concatenate(
        [(np.arange(LANES)[:, None] == lane[None, :]) for lane in lanes], axis=1
    ).astype(ml_dtypes.bfloat16)


def swap_pairs(rows):
    size = rows.shape[-2]
    axis = rows.ndim - 2
    even = lax.broadcasted_iota(jnp.int32, rows.shape, axis) % 2 == 0
    return jnp.where(
        even, pltpu.roll(rows, size - 1, axis), pltpu.roll(rows, 1, axis)
    ), even


def halves_swapped(rows):
    half = rows.shape[0] // 2
    return jnp.concatenate([rows[half:], rows[:half]], axis=0)


def kernel(
    dims,
    spectra_hbm,
    valid_hbm,
    partner_hbm,
    bin_hbm,
    count_hbm,
    expand_hbm,
    table_hbm,
    phase_hbm,
    out_ref,
    own,
    valid_ref,
    partner_ref,
    bin_ref,
    count_ref,
    expand_ref,
    meta_ref,
    metas,
    white,
    plain,
    same,
    odd,
    plain_turn,
    odd_turn,
    table,
    phases,
    cross_bins,
    select_re,
    select_im,
    cross_re,
    cross_im,
    products,
    cross_products,
    total_re,
    total_im,
    outgoing,
    incoming,
    local_sems,
    send_a,
    recv_a,
    send_m,
    recv_m,
    send_b,
    recv_b,
    ready,
    token,
):
    n, nchan, nwin, nfreq, nbins_dev = dims
    nrow = nchan * nwin * 2
    nbins = n * nbins_dev
    npairs = nchan * nchan
    ngroups = n // GROUP
    half = n // 2
    me = lax.axis_index("chan")

    def peer(k):
        bits = range((n - 1).bit_length())
        return sum((me // 2**b + k // 2**b) % 2 * 2**b for b in bits)

    def remote(src, dst, send, recv, target):
        return pltpu.make_async_remote_copy(
            src_ref=src,
            dst_ref=dst,
            send_sem=send,
            recv_sem=recv,
            device_id={"chan": target},
            device_id_type=pl.DeviceIdType.MESH,
        )

    def span(buffer, first, count, send, recv):
        part = buffer.at[pl.ds(first, count)]
        return remote(part, part, send, recv, peer(1))

    copy_own = pltpu.make_async_copy(spectra_hbm, own, local_sems.at[0])
    copy_table = pltpu.make_async_copy(table_hbm, table, local_sems.at[1])
    copy_phase = pltpu.make_async_copy(phase_hbm, phases, local_sems.at[2])
    small = [
        pltpu.make_async_copy(src, dst, local_sems.at[3 + i])
        for i, (src, dst) in enumerate(
            (
                (valid_hbm, valid_ref),
                (bin_hbm, bin_ref),
                (count_hbm, count_ref),
                (partner_hbm, partner_ref),
                (expand_hbm, expand_ref),
            )
        )
    ]
    copy_own.start()
    for copy in small[:3]:
        copy.start()
    plane = me // PLANE
    is_last = plane == n // PLANE - 1
    barrier = pltpu.get_barrier_semaphore()

    def signal(sem, ks):
        for k in ks:
            pl.semaphore_signal(
                sem,
                inc=1,
                device_id={"chan": peer(k)},
                device_id_type=pl.DeviceIdType.MESH,
            )

    @pl.when(jnp.logical_not(is_last))
    def _():
        signal(barrier, range(n - 1, 0, -1))

    for copy in small[3:]:
        copy.start()
    copy_table.start()
    copy_phase.start()
    for copy in small[:3]:
        copy.wait()

    lane = lax.broadcasted_iota(jnp.int32, meta_ref.shape, 1)
    bins = jnp.full(meta_ref.shape, -1, jnp.int32)
    for row in range(2 * npairs):
        bins = jnp.where(lane == row, bin_ref[row], bins)
    bins = jnp.where((lane < count_ref[0]) & (bins >= 0), bins, -1)
    meta_ref[...] = bins

    sub = lax.broadcasted_iota(jnp.int32, (nchan, 2 * nwin, LANES), 1) // 2
    chan = lax.broadcasted_iota(jnp.int32, (nchan, 2 * nwin, LANES), 0)
    usable = jnp.zeros((nchan, 2 * nwin, LANES), jnp.float32)
    for c in range(nchan):
        for w in range(nwin):
            usable = jnp.where(
                (chan == c) & (sub == w), valid_ref[c, w].astype(jnp.float32), usable
            )

    def whiten_slice(t):
        here = pl.ds(pl.multiple_of(t * nfreq, nfreq), nfreq)
        x = own[:, :, :, here].astype(jnp.float32)
        x = x.reshape(nchan, 2 * nwin, nfreq)
        swapped, _ = swap_pairs(x)
        power = x * x + swapped * swapped
        for b in range(nfreq // BAND):
            band = slice(b * BAND, (b + 1) * BAND)
            total = jnp.sum(power[:, :, band], axis=-1, keepdims=True)
            scale = lax.rsqrt(total * (1.0 / BAND) + 1e-06) * usable
            rows = (x[:, :, band] * scale).reshape(nrow, BAND)
            white[t, :, band] = rows.astype(jnp.bfloat16)

    def send_meta(k):
        remote(meta_ref, metas.at[k], send_m, recv_m.at[k // half], peer(k)).start()

    def send_white(k):
        remote(white.at[peer(k)], plain.at[k], send_a, recv_a.at[k // GROUP], peer(k)).start()

    def each(act, ks):
        for k in ks:
            act(k)

    near = [7, 6, 5, 4]
    middle = [11, 10, 9, 8]
    far = [15, 14, 13, 12]
    inside = [3, 2, 1]
    copy_own.wait()

    @pl.when(jnp.logical_not(is_last))
    def _():
        def step(i, carry):
            for u in range(4):
                whiten_slice(4 * i + u)
            return carry

        lax.fori_loop(0, n // 4, step, 0)
        pl.semaphore_wait(barrier, 3 * PLANE - 1)

    @pl.when(is_last)
    def _():
        pl.semaphore_wait(barrier, 3 * PLANE)
        signal(ready, far + middle + near)
        each(send_meta, far + middle + near)
        for k in far + middle + near:
            whiten_slice(peer(k))
            send_white(k)
        for k in [*inside, 0]:
            whiten_slice(peer(k))
        pl.semaphore_wait(token, 1)
        each(send_meta, inside)
        each(send_white, inside)

    @pl.when(plane == 2)
    def _():
        each(send_meta, far + middle + inside)
        each(send_white, far + middle)
        pl.semaphore_wait(ready, PLANE)
        signal(token, near[-1:])
        each(send_meta, near)
        each(send_white, near + inside)

    @pl.when(plane == 1)
    def _():
        each(send_meta, far + near + inside)
        each(send_white, far + near)
        pl.semaphore_wait(ready, PLANE)
        each(send_meta, middle)
        each(send_white, middle + inside)

    @pl.when(plane == 0)
    def _():
        each(send_meta, middle + near + inside)
        each(send_white, middle)
        pl.semaphore_wait(ready, PLANE)
        each(send_meta, far)
        each(send_white, far + near + inside)

    plain[0] = white[me]
    metas[0] = meta_ref[...]
    for copy in small[3:]:
        copy.wait()
    mirror = partner_ref[0]
    across = mirror // PLANE
    lead = jnp.where(across == 2, 1, 0)
    early, late = [], []
    for j in range(PLANE):
        inner = jnp.where(mirror == 2, j % 2, j % 2 * 2)
        early.append(jnp.where(across == 0, j // 2 * PLANE + inner, lead * PLANE + j))
        late.append(jnp.where(across == 0, (3 - j // 2) * PLANE + inner, 2 * PLANE + j))
    firsts = early + late
    sequence = [0, 1, 3, 2]

    def prepare(k):
        same[k] = plain[k]
        x = plain[k].astype(jnp.float32)
        swapped, even = swap_pairs(x)
        turn = jnp.where(even, -swapped, swapped)
        step = 2 * nwin
        odd[k] = jnp.concatenate([x[step:], x[:step]], axis=0).astype(jnp.bfloat16)
        plain_turn[k] = turn.astype(jnp.bfloat16)
        odd_turn[k] = jnp.concatenate([turn[step:], turn[:step]], axis=0).astype(jnp.bfloat16)

    def put(target, at, left, right, right_turn):
        target[pl.ds(at, nrow), 0:nfreq] = left * right
        target[pl.ds(at, nrow), nfreq : 2 * nfreq] = left * right_turn

    def multiply_self(target, g):
        for u in range(GROUP):
            k = g * GROUP + u
            x = plain[k]
            xt = plain_turn[k]
            put(target, u * nrow, x, x, xt)
            put(target, LANES + u * nrow, x, odd[k], odd_turn[k])
            put(target, 2 * LANES + u * nrow, x, halves_swapped(x), halves_swapped(xt))

    base = 3 * LANES

    bin_rows = lax.broadcasted_iota(jnp.int32, (nbins, LANES), 0)
    bin_rows = bin_rows.astype(jnp.float32).astype(jnp.bfloat16)
    one = jnp.ones((nbins, LANES), jnp.bfloat16)
    zero = jnp.zeros((nbins, LANES), jnp.bfloat16)

    def one_hot(row):
        return jnp.where(bin_rows == row.astype(jnp.bfloat16), one, zero)

    def select_self(part):
        first = part * half
        count = half - (part == 0)
        span(metas, first + (part == 0), count, send_m, recv_m.at[part]).wait_recv()
        spread = jnp.dot(
            metas[first : first + half, 0, :].astype(jnp.float32).astype(jnp.bfloat16),
            expand_ref[...],
            preferred_element_type=jnp.float32,
        )
        for u in range(half):
            cross_bins[first + u, 0:1, :] = spread[u : u + 1, 4 * LANES : 5 * LANES]
            cross_bins[first + u, 1:2, :] = spread[u : u + 1, 5 * LANES : 6 * LANES]
        self_bins = spread[:, : 4 * LANES]
        slot = lax.broadcasted_iota(jnp.int32, self_bins.shape, 0) % GROUP
        place = lax.broadcasted_iota(jnp.int32, self_bins.shape, 1) % LANES // nrow
        self_bins = jnp.where(slot == place, self_bins, 0.0)
        for v in range(half // GROUP):
            i = sequence.index(part * half // GROUP + v)
            row = jnp.sum(self_bins[v * GROUP : (v + 1) * GROUP], axis=0, keepdims=True)
            alone, ahead, back, over = [
                one_hot(row[:, h * LANES : (h + 1) * LANES]) for h in range(4)
            ]
            at = i * base
            for target, mixed in ((select_re, ahead + back), (select_im, ahead - back)):
                target[:, at : at + LANES] = alone
                target[:, at + LANES : at + 2 * LANES] = mixed
                target[:, at + 2 * LANES : at + 3 * LANES] = over

    def select_cross():
        for j in range(n // 2):
            ahead = one_hot(cross_bins[firsts[j], 0:1, :])
            back = one_hot(cross_bins[firsts[j] ^ mirror, 1:2, :])
            cross_re[:, j * LANES : (j + 1) * LANES] = ahead + back
            cross_im[:, j * LANES : (j + 1) * LANES] = ahead - back

    def product(left, right):
        return jnp.dot(left, right, preferred_element_type=jnp.float32)

    def multiply_cross(j):
        x = same[firsts[j]]
        q = firsts[j] ^ mirror
        at = j * LANES
        y, yt, z, zt = same[q], plain_turn[q], odd[q], odd_turn[q]
        put(cross_products, at, x, y, yt)
        put(cross_products, at + nrow, x, z, zt)
        put(cross_products, at + 2 * nrow, x, halves_swapped(y), halves_swapped(yt))
        put(cross_products, at + 3 * nrow, x, halves_swapped(z), halves_swapped(zt))

    def cross_sum(selector, first, last, columns):
        rows = slice(first * LANES, last * LANES)
        return product(selector[:, rows], cross_products[rows, columns])

    def self_sum(selector, i, columns):
        return product(selector[:, i * base : (i + 1) * base], products[i % 2, :, columns])

    real, imag = slice(0, nfreq), slice(nfreq, 2 * nfreq)
    def collect(i):
        g = sequence[i]
        here = range(max(g * GROUP, 1), (g + 1) * GROUP)
        span(plain, here[0], len(here), send_a, recv_a.at[g]).wait_recv()
        for k in range(g * GROUP, (g + 1) * GROUP):
            prepare(k)
        multiply_self(products.at[i % 2], g)

    collect(0)
    collect(1)
    select_self(0)
    total_re[...] = self_sum(select_re, 0, real) + self_sum(select_re, 1, real)
    total_im[...] = self_sum(select_im, 0, imag) + self_sum(select_im, 1, imag)
    select_self(1)
    select_cross()
    collect(2)
    for j in range(PLANE):
        multiply_cross(j)
    total_re[...] += self_sum(select_re, 2, real) + cross_sum(cross_re, 0, PLANE, real)
    total_im[...] += self_sum(select_im, 2, imag) + cross_sum(cross_im, 0, PLANE, imag)
    collect(3)
    for j in range(PLANE, 2 * PLANE):
        multiply_cross(j)
    last = ngroups - 1
    terms_re = (
        total_re[...]
        + self_sum(select_re, last, real)
        + cross_sum(cross_re, PLANE, 2 * PLANE, real)
    )
    terms_re = terms_re.reshape(n, nbins_dev, nfreq).astype(jnp.bfloat16)
    terms_im = (
        total_im[...]
        + self_sum(select_im, last, imag)
        + cross_sum(cross_im, PLANE, 2 * PLANE, imag)
    )
    terms_im = terms_im.reshape(n, nbins_dev, nfreq).astype(jnp.bfloat16)
    outgoing[:, :, real] = terms_re
    outgoing[:, :, imag] = terms_im

    for i in range(n - 1):
        target = i + (i + n - me) // n
        remote(outgoing.at[target], incoming.at[me], send_b, recv_b, target).start()
    incoming[me] = outgoing[me]
    copy_table.wait()
    copy_phase.wait()
    span(incoming, 0, n - 1, send_b, recv_b).wait_recv()

    stacked = incoming[...].astype(jnp.float32).reshape(nbins, 2 * nfreq).astype(jnp.bfloat16)
    lags = product(stacked, table[...])
    lags = jnp.sum(lags.reshape(n, nbins_dev, 2 * LAGS) * phases[...], axis=0)
    out_ref[...] = lags[:, :LAGS] + lags[:, LAGS:]

    span(metas, 1, n - 1, send_m, recv_m.at[0]).wait_send()
    span(plain, 1, n - 1, send_a, recv_a.at[0]).wait_send()
    span(incoming, 0, n - 1, send_b, recv_b).wait_send()


def on_device_slices(spectra, valid, partner, pair_bin, pair_count):
    n = lax.axis_size("chan")
    nchan, nwin, _, nfreq_all = spectra.shape
    nfreq = nfreq_all // n
    nrow = nchan * nwin * 2
    nbins = n * BINS_DEV
    base = 3 * LANES
    deep = n // 2 * LANES
    scale = 1.0 / (math.sqrt(nfreq_all) * nwin * math.sqrt(PAIRS_DEV // BINS_DEV))
    hbm = pl.BlockSpec(memory_space=pltpu.HBM)
    vmem = pl.BlockSpec(memory_space=pltpu.VMEM)
    dma = pltpu.SemaphoreType.DMA
    bf16 = jnp.bfloat16
    return pl.pallas_call(
        functools.partial(kernel, (n, nchan, nwin, nfreq, BINS_DEV)),
        out_shape=pltpu.VMEM((BINS_DEV, LAGS), jnp.float32),
        in_specs=[hbm] * 8,
        out_specs=vmem,
        scratch_shapes=[
            pltpu.VMEM(spectra.shape, bf16),
            pltpu.SMEM(valid.shape, jnp.int32),
            pltpu.SMEM(partner.shape, jnp.int32),
            pltpu.SMEM(pair_bin.shape, jnp.int32),
            pltpu.SMEM(pair_count.shape, jnp.int32),
            pltpu.VMEM((LANES, 6 * LANES), bf16),
            pltpu.VMEM((1, LANES), jnp.int32),
            pltpu.VMEM((n, 1, LANES), jnp.int32),
            pltpu.VMEM((n, nrow, nfreq), bf16),
            pltpu.VMEM((n, nrow, nfreq), bf16),
            pltpu.VMEM((n, nrow, nfreq), bf16),
            pltpu.VMEM((n, nrow, nfreq), bf16),
            pltpu.VMEM((n, nrow, nfreq), bf16),
            pltpu.VMEM((n, nrow, nfreq), bf16),
            pltpu.VMEM((2 * nfreq, 2 * LAGS), bf16),
            pltpu.VMEM((n, 1, 2 * LAGS), jnp.float32),
            pltpu.VMEM((n, 8, LANES), jnp.float32),
            pltpu.VMEM((nbins, n // GROUP * base), bf16),
            pltpu.VMEM((nbins, n // GROUP * base), bf16),
            pltpu.VMEM((nbins, deep), bf16),
            pltpu.VMEM((nbins, deep), bf16),
            pltpu.VMEM((2, base, 2 * nfreq), bf16),
            pltpu.VMEM((deep, 2 * nfreq), bf16),
            pltpu.VMEM((nbins, nfreq), jnp.float32),
            pltpu.VMEM((nbins, nfreq), jnp.float32),
            pltpu.VMEM((n, BINS_DEV, 2 * nfreq), bf16),
            pltpu.VMEM((n, BINS_DEV, 2 * nfreq), bf16),
            dma((8,)),
            dma,
            dma((n // GROUP,)),
            dma,
            dma((2,)),
            dma,
            dma,
            pltpu.SemaphoreType.REGULAR,
            pltpu.SemaphoreType.REGULAR,
        ],
        compiler_params=pltpu.CompilerParams(
            collective_id=0, has_side_effects=True, vmem_limit_bytes=60 * 1024 * 1024
        ),
    )(
        spectra,
        valid,
        partner,
        pair_bin,
        pair_count,
        jnp.asarray(expanders(nchan, nwin)),
        jnp.asarray(base_table(nfreq)),
        jnp.asarray(slice_phases(n, nfreq, scale)),
    )


def solution(mesh):
    in_specs = (
        P(("grp", "chan"), None, None, None),
        P(("grp", "chan"), None),
        P(),
        P(("grp", "chan")),
        P(("grp", "chan")),
    )
    out_specs = P(("grp", "chan"), None)
    nblocks = mesh.shape["chan"]
    whole_bands = F % (nblocks * BAND) == 0 and nblocks == GROUP * PLANE
    return jax.shard_map(
        on_device_slices if whole_bands else on_device_blocks,
        mesh=mesh,
        in_specs=in_specs,
        out_specs=out_specs,
        check_vma=False,
    )
```

```python
import functools
import math

import jax
import jax.numpy as jnp
import ml_dtypes
import numpy as np
from jax import lax
from jax.experimental import pallas as pl
from jax.experimental.pallas import tpu as pltpu
from jax.sharding import PartitionSpec as P

F = 4096
BAND = 128
LAGS = 1024
BINS_DEV = 8
PAIRS_DEV = 32
LANES = 128
GROUP = 4
PLANE = 4


def from_partner(block, axis, bit):
    count = lax.axis_size(axis)
    route = []
    for low in range(count):
        high = low | 1 << bit
        if high != low and high < count:
            route += [(low, high), (high, low)]
    return lax.ppermute(block, axis, route)


def whiten(spectra, valid):
    values = spectra.astype(jnp.float32)
    power = values[:, :, 0] * values[:, :, 0] + values[:, :, 1] * values[:, :, 1]
    nchan, nwin, nfreq = power.shape
    banded = jnp.mean(power.reshape(nchan, nwin, nfreq // BAND, BAND), axis=-1)
    amplitude = jnp.repeat(jnp.sqrt(banded + 1e-06), BAND, axis=-1)
    weights = valid.astype(jnp.float32)[:, :, None, None]
    return (values * weights / amplitude[:, :, None, :]).astype(jnp.bfloat16)


def lag_table():
    freqs = jnp.arange(F, dtype=jnp.int32)
    shifts = jnp.arange(LAGS, dtype=jnp.int32) - LAGS // 2
    phase = jnp.mod(freqs[:, None] * shifts[None, :], 2 * F)
    angle = phase.astype(jnp.float32) * (2.0 * math.pi / (2 * F))
    scale = 1.0 / math.sqrt(F)
    return jnp.concatenate([jnp.cos(angle) * scale, -jnp.sin(angle) * scale], axis=0).astype(
        jnp.bfloat16
    )


def cross_product(left_part, right_part):
    return jnp.einsum("awf,bwf->abf", left_part, right_part, preferred_element_type=jnp.float32)


def correlate(own_block, other_block, table):
    own_real = own_block[:, :, 0]
    own_imag = own_block[:, :, 1]
    oth_real = other_block[:, :, 0]
    oth_imag = other_block[:, :, 1]
    real_part = cross_product(own_real, oth_real) + cross_product(own_imag, oth_imag)
    imag_part = cross_product(own_imag, oth_real) - cross_product(own_real, oth_imag)
    nchan = own_block.shape[0]
    nwin = own_block.shape[1]
    spec = (jnp.concatenate([real_part, imag_part], axis=-1) * (1.0 / nwin)).reshape(
        nchan * nchan, -1
    )
    spec = spec.astype(jnp.bfloat16)
    return jnp.dot(spec, table, preferred_element_type=jnp.float32)


def select_sum(selector, corr_high, corr_low):
    return jnp.dot(selector, corr_high, preferred_element_type=jnp.float32) + jnp.dot(
        selector, corr_low, preferred_element_type=jnp.float32
    )


def on_device_blocks(spectra, valid, partner, pair_bin, pair_count):
    white = whiten(spectra, valid)
    nblocks = lax.axis_size("chan")
    round_mask = partner[0]
    paired = white
    for bit_index in range(nblocks.bit_length() - 1):
        swapped = from_partner(paired, "chan", bit_index)
        paired = jnp.where(round_mask >> bit_index & 1 == 1, swapped, paired)
    table = lag_table()
    self_corr = correlate(white, white, table)
    cross_corr = correlate(white, paired, table)
    corr = jnp.concatenate([self_corr, cross_corr], axis=0)
    corr_high = corr.astype(jnp.bfloat16)
    corr_low = (corr - corr_high.astype(jnp.float32)).astype(jnp.bfloat16)
    rows = jnp.arange(corr.shape[0], dtype=jnp.int32)
    live_rows = (rows < pair_count[0]) & (pair_bin >= 0)
    kept_bins = jnp.where(live_rows, pair_bin, -1)
    targets = lax.iota(jnp.int32, nblocks * BINS_DEV)
    selector = (kept_bins[None, :] == targets[:, None]).astype(jnp.bfloat16)
    terms = select_sum(selector, corr_high, corr_low).reshape(nblocks, BINS_DEV, -1)
    received = lax.all_to_all(terms, "chan", split_axis=0, concat_axis=0, tiled=True)
    summed = jnp.sum(received, axis=0)
    return summed * (1.0 / math.sqrt(PAIRS_DEV // BINS_DEV))


def lag_span():
    return LAGS // 2 + LANES


def interleaved(cos, sin):
    tiled = [part.reshape(part.shape[0], -1, 1, LANES) for part in (cos, sin)]
    return np.concatenate(tiled, axis=2).reshape(cos.shape[0], -1)


def base_table(nfreq):
    shifts = np.arange(lag_span())
    angle = np.mod(np.arange(nfreq)[:, None] * shifts[None, :], 2 * F) * (2.0 * math.pi / (2 * F))
    return interleaved(np.cos(angle), np.sin(angle)).astype(ml_dtypes.bfloat16)


def slice_phases(nslices, nfreq, scale):
    shifts = np.arange(lag_span())
    first = np.arange(nslices) * nfreq
    angle = np.mod(first[:, None] * shifts[None, :], 2 * F) * (2.0 * math.pi / (2 * F))
    both = interleaved(np.cos(angle), np.sin(angle)) * scale
    return both.astype(np.float32)[:, None, :]


def expanders(nchan, nwin):
    row = np.arange(LANES)
    per_chan = 2 * nwin
    chan = row // per_chan % nchan
    shift = row // (per_chan * nchan)
    npairs = nchan * nchan

    def pair(step):
        return chan * nchan + (chan + step) % nchan

    def reverse(step):
        return (chan + step) % nchan * nchan + chan

    lanes = (
        pair(0),
        pair(1),
        reverse(1),
        pair(2),
        npairs + pair(shift),
        npairs + reverse(shift),
    )
    return np.concatenate(
        [(np.arange(LANES)[:, None] == lane[None, :]) for lane in lanes], axis=1
    ).astype(ml_dtypes.bfloat16)


def swap_pairs(rows):
    size = rows.shape[-2]
    axis = rows.ndim - 2
    even = lax.broadcasted_iota(jnp.int32, rows.shape, axis) % 2 == 0
    return jnp.where(
        even, pltpu.roll(rows, size - 1, axis), pltpu.roll(rows, 1, axis)
    ), even


def halves_swapped(rows):
    half = rows.shape[0] // 2
    return jnp.concatenate([rows[half:], rows[:half]], axis=0)


def kernel(
    dims,
    spectra_hbm,
    valid_hbm,
    partner_hbm,
    bin_hbm,
    count_hbm,
    expand_hbm,
    table_hbm,
    phase_hbm,
    out_ref,
    own,
    valid_ref,
    partner_ref,
    bin_ref,
    count_ref,
    expand_ref,
    meta_ref,
    metas,
    white,
    plain,
    same,
    odd,
    plain_turn,
    odd_turn,
    table,
    phases,
    cross_bins,
    select_re,
    select_im,
    cross_re,
    cross_im,
    products,
    cross_products,
    total_re,
    total_im,
    outgoing,
    incoming,
    local_sems,
    send_a,
    recv_a,
    send_m,
    recv_m,
    send_b,
    recv_b,
    ready,
    token,
):
    n, nchan, nwin, nfreq, nbins_dev = dims
    nrow = nchan * nwin * 2
    nbins = n * nbins_dev
    npairs = nchan * nchan
    ngroups = n // GROUP
    half = n // 2
    me = lax.axis_index("chan")

    def peer(k):
        bits = range((n - 1).bit_length())
        return sum((me // 2**b + k // 2**b) % 2 * 2**b for b in bits)

    def remote(src, dst, send, recv, target):
        return pltpu.make_async_remote_copy(
            src_ref=src,
            dst_ref=dst,
            send_sem=send,
            recv_sem=recv,
            device_id={"chan": target},
            device_id_type=pl.DeviceIdType.MESH,
        )

    def span(buffer, first, count, send, recv):
        part = buffer.at[pl.ds(first, count)]
        return remote(part, part, send, recv, peer(1))

    copy_own = pltpu.make_async_copy(spectra_hbm, own, local_sems.at[0])
    copy_table = pltpu.make_async_copy(table_hbm, table, local_sems.at[1])
    copy_phase = pltpu.make_async_copy(phase_hbm, phases, local_sems.at[2])
    small = [
        pltpu.make_async_copy(src, dst, local_sems.at[3 + i])
        for i, (src, dst) in enumerate(
            (
                (valid_hbm, valid_ref),
                (bin_hbm, bin_ref),
                (count_hbm, count_ref),
                (partner_hbm, partner_ref),
                (expand_hbm, expand_ref),
            )
        )
    ]
    copy_own.start()
    for copy in small[:3]:
        copy.start()
    plane = me // PLANE
    is_last = plane == n // PLANE - 1
    barrier = pltpu.get_barrier_semaphore()

    def signal(sem, ks):
        for k in ks:
            pl.semaphore_signal(
                sem,
                inc=1,
                device_id={"chan": peer(k)},
                device_id_type=pl.DeviceIdType.MESH,
            )

    @pl.when(jnp.logical_not(is_last))
    def _():
        signal(barrier, range(n - 1, 0, -1))

    for copy in small[3:]:
        copy.start()
    copy_table.start()
    copy_phase.start()
    for copy in small[:3]:
        copy.wait()

    lane = lax.broadcasted_iota(jnp.int32, meta_ref.shape, 1)
    bins = jnp.full(meta_ref.shape, -1, jnp.int32)
    for row in range(2 * npairs):
        bins = jnp.where(lane == row, bin_ref[row], bins)
    bins = jnp.where((lane < count_ref[0]) & (bins >= 0), bins, -1)
    meta_ref[...] = bins

    sub = lax.broadcasted_iota(jnp.int32, (nchan, 2 * nwin, LANES), 1) // 2
    chan = lax.broadcasted_iota(jnp.int32, (nchan, 2 * nwin, LANES), 0)
    usable = jnp.zeros((nchan, 2 * nwin, LANES), jnp.float32)
    for c in range(nchan):
        for w in range(nwin):
            usable = jnp.where(
                (chan == c) & (sub == w), valid_ref[c, w].astype(jnp.float32), usable
            )

    def whiten_slice(t):
        here = pl.ds(pl.multiple_of(t * nfreq, nfreq), nfreq)
        x = own[:, :, :, here].astype(jnp.float32)
        x = x.reshape(nchan, 2 * nwin, nfreq)
        swapped, _ = swap_pairs(x)
        power = x * x + swapped * swapped
        for b in range(nfreq // BAND):
            band = slice(b * BAND, (b + 1) * BAND)
            total = jnp.sum(power[:, :, band], axis=-1, keepdims=True)
            scale = lax.rsqrt(total * (1.0 / BAND) + 1e-06) * usable
            rows = (x[:, :, band] * scale).reshape(nrow, BAND)
            white[t, :, band] = rows.astype(jnp.bfloat16)

    def send_meta(k):
        remote(meta_ref, metas.at[k], send_m, recv_m.at[k // half], peer(k)).start()

    def send_white(k):
        remote(white.at[peer(k)], plain.at[k], send_a, recv_a.at[k // GROUP], peer(k)).start()

    def each(act, ks):
        for k in ks:
            act(k)

    near = [7, 6, 5, 4]
    middle = [11, 10, 9, 8]
    far = [15, 14, 13, 12]
    inside = [3, 2, 1]
    copy_own.wait()

    @pl.when(jnp.logical_not(is_last))
    def _():
        def step(i, carry):
            for u in range(4):
                whiten_slice(4 * i + u)
            return carry

        lax.fori_loop(0, n // 4, step, 0)
        pl.semaphore_wait(barrier, 3 * PLANE - 1)

    @pl.when(is_last)
    def _():
        pl.semaphore_wait(barrier, 3 * PLANE)
        signal(ready, far + middle + near)
        each(send_meta, far + middle + near)
        for k in far + middle + near:
            whiten_slice(peer(k))
            send_white(k)
        for k in [*inside, 0]:
            whiten_slice(peer(k))
        pl.semaphore_wait(token, 1)
        each(send_meta, inside)
        each(send_white, inside)

    @pl.when(plane == 2)
    def _():
        each(send_meta, far + middle + inside)
        each(send_white, far + middle)
        pl.semaphore_wait(ready, PLANE)
        signal(token, near[-1:])
        each(send_meta, near)
        each(send_white, near + inside)

    @pl.when(plane == 1)
    def _():
        each(send_meta, far + near + inside)
        each(send_white, far + near)
        pl.semaphore_wait(ready, PLANE)
        each(send_meta, middle)
        each(send_white, middle + inside)

    @pl.when(plane == 0)
    def _():
        each(send_meta, middle + near + inside)
        each(send_white, middle)
        pl.semaphore_wait(ready, PLANE)
        each(send_meta, far)
        each(send_white, far + near + inside)

    plain[0] = white[me]
    metas[0] = meta_ref[...]
    for copy in small[3:]:
        copy.wait()
    mirror = partner_ref[0]
    across = mirror // PLANE
    lead = jnp.where(across == 2, 1, 0)
    early, late = [], []
    for j in range(PLANE):
        inner = jnp.where(mirror == 2, j % 2, j % 2 * 2)
        early.append(jnp.where(across == 0, j // 2 * PLANE + inner, lead * PLANE + j))
        late.append(jnp.where(across == 0, (3 - j // 2) * PLANE + inner, 2 * PLANE + j))
    firsts = early + late
    sequence = [0, 1, 3, 2]

    def prepare(k):
        same[k] = plain[k]
        x = plain[k].astype(jnp.float32)
        swapped, even = swap_pairs(x)
        turn = jnp.where(even, -swapped, swapped)
        step = 2 * nwin
        odd[k] = jnp.concatenate([x[step:], x[:step]], axis=0).astype(jnp.bfloat16)
        plain_turn[k] = turn.astype(jnp.bfloat16)
        odd_turn[k] = jnp.concatenate([turn[step:], turn[:step]], axis=0).astype(jnp.bfloat16)

    def put(target, at, left, right, right_turn):
        target[pl.ds(at, nrow), 0:nfreq] = left * right
        target[pl.ds(at, nrow), nfreq : 2 * nfreq] = left * right_turn

    def multiply_self(target, g):
        for u in range(GROUP):
            k = g * GROUP + u
            x = plain[k]
            xt = plain_turn[k]
            put(target, u * nrow, x, x, xt)
            put(target, LANES + u * nrow, x, odd[k], odd_turn[k])
            put(target, 2 * LANES + u * nrow, x, halves_swapped(x), halves_swapped(xt))

    base = 3 * LANES

    bin_rows = lax.broadcasted_iota(jnp.int32, (nbins, LANES), 0)
    bin_rows = bin_rows.astype(jnp.float32).astype(jnp.bfloat16)
    one = jnp.ones((nbins, LANES), jnp.bfloat16)
    zero = jnp.zeros((nbins, LANES), jnp.bfloat16)

    def one_hot(row):
        return jnp.where(bin_rows == row.astype(jnp.bfloat16), one, zero)

    def select_self(part):
        first = part * half
        count = half - (part == 0)
        span(metas, first + (part == 0), count, send_m, recv_m.at[part]).wait_recv()
        spread = jnp.dot(
            metas[first : first + half, 0, :].astype(jnp.float32).astype(jnp.bfloat16),
            expand_ref[...],
            preferred_element_type=jnp.float32,
        )
        for u in range(half):
            cross_bins[first + u, 0:1, :] = spread[u : u + 1, 4 * LANES : 5 * LANES]
            cross_bins[first + u, 1:2, :] = spread[u : u + 1, 5 * LANES : 6 * LANES]
        self_bins = spread[:, : 4 * LANES]
        slot = lax.broadcasted_iota(jnp.int32, self_bins.shape, 0) % GROUP
        place = lax.broadcasted_iota(jnp.int32, self_bins.shape, 1) % LANES // nrow
        self_bins = jnp.where(slot == place, self_bins, 0.0)
        for v in range(half // GROUP):
            i = sequence.index(part * half // GROUP + v)
            row = jnp.sum(self_bins[v * GROUP : (v + 1) * GROUP], axis=0, keepdims=True)
            alone, ahead, back, over = [
                one_hot(row[:, h * LANES : (h + 1) * LANES]) for h in range(4)
            ]
            at = i * base
            for target, mixed in ((select_re, ahead + back), (select_im, ahead - back)):
                target[:, at : at + LANES] = alone
                target[:, at + LANES : at + 2 * LANES] = mixed
                target[:, at + 2 * LANES : at + 3 * LANES] = over

    def select_cross():
        for j in range(n // 2):
            ahead = one_hot(cross_bins[firsts[j], 0:1, :])
            back = one_hot(cross_bins[firsts[j] ^ mirror, 1:2, :])
            cross_re[:, j * LANES : (j + 1) * LANES] = ahead + back
            cross_im[:, j * LANES : (j + 1) * LANES] = ahead - back

    def product(left, right):
        return jnp.dot(left, right, preferred_element_type=jnp.float32)

    def multiply_cross(j):
        x = same[firsts[j]]
        q = firsts[j] ^ mirror
        at = j * LANES
        y, yt, z, zt = same[q], plain_turn[q], odd[q], odd_turn[q]
        put(cross_products, at, x, y, yt)
        put(cross_products, at + nrow, x, z, zt)
        put(cross_products, at + 2 * nrow, x, halves_swapped(y), halves_swapped(yt))
        put(cross_products, at + 3 * nrow, x, halves_swapped(z), halves_swapped(zt))

    def cross_sum(selector, first, last, columns):
        rows = slice(first * LANES, last * LANES)
        return product(selector[:, rows], cross_products[rows, columns])

    def self_sum(selector, i, columns):
        return product(selector[:, i * base : (i + 1) * base], products[i % 2, :, columns])

    real, imag = slice(0, nfreq), slice(nfreq, 2 * nfreq)
    def collect(i):
        g = sequence[i]
        here = range(max(g * GROUP, 1), (g + 1) * GROUP)
        span(plain, here[0], len(here), send_a, recv_a.at[g]).wait_recv()
        for k in range(g * GROUP, (g + 1) * GROUP):
            prepare(k)
        multiply_self(products.at[i % 2], g)

    collect(0)
    collect(1)
    select_self(0)
    total_re[...] = self_sum(select_re, 0, real) + self_sum(select_re, 1, real)
    total_im[...] = self_sum(select_im, 0, imag) + self_sum(select_im, 1, imag)
    select_self(1)
    select_cross()
    collect(2)
    for j in range(PLANE):
        multiply_cross(j)
    total_re[...] += self_sum(select_re, 2, real) + cross_sum(cross_re, 0, PLANE, real)
    total_im[...] += self_sum(select_im, 2, imag) + cross_sum(cross_im, 0, PLANE, imag)
    collect(3)
    for j in range(PLANE, 2 * PLANE):
        multiply_cross(j)
    last = ngroups - 1
    terms_re = (
        total_re[...]
        + self_sum(select_re, last, real)
        + cross_sum(cross_re, PLANE, 2 * PLANE, real)
    )
    terms_re = terms_re.reshape(n, nbins_dev, nfreq).astype(jnp.bfloat16)
    terms_im = (
        total_im[...]
        + self_sum(select_im, last, imag)
        + cross_sum(cross_im, PLANE, 2 * PLANE, imag)
    )
    terms_im = terms_im.reshape(n, nbins_dev, nfreq).astype(jnp.bfloat16)
    outgoing[:, :, real] = terms_re
    outgoing[:, :, imag] = terms_im

    for i in range(n - 1):
        target = i + (i + n - me) // n
        remote(outgoing.at[target], incoming.at[me], send_b, recv_b, target).start()
    incoming[me] = outgoing[me]
    copy_table.wait()
    copy_phase.wait()
    span(incoming, 0, n - 1, send_b, recv_b).wait_recv()

    arrived = incoming[...].astype(jnp.float32).reshape(nbins, 2 * nfreq).astype(jnp.bfloat16)
    stacked = jnp.concatenate([arrived[:, real], arrived[:, imag]], axis=0)
    zero_lag = LAGS // 2
    lane = lax.broadcasted_iota(jnp.int32, (nbins_dev, LANES), 1)
    backward = (LANES - lane) % LANES
    mirrored = []
    for a in range(lag_span() // LANES):
        both = slice(2 * a * LANES, 2 * (a + 1) * LANES)
        lags = product(stacked, table[:, both]).reshape(2, n, nbins_dev, 2 * LANES)
        cos, sin = phases[:, :, both][:, :, :LANES], phases[:, :, both][:, :, LANES:]
        even_part = jnp.sum(lags[0, :, :, :LANES] * cos - lags[0, :, :, LANES:] * sin, axis=0)
        odd_part = jnp.sum(lags[1, :, :, LANES:] * cos + lags[1, :, :, :LANES] * sin, axis=0)
        if a < zero_lag // LANES:
            out_ref[:, zero_lag + a * LANES : zero_lag + (a + 1) * LANES] = even_part - odd_part
        mirrored.append(even_part + odd_part)
    for a in range(zero_lag // LANES):
        high = mirrored[zero_lag // LANES - a]
        low = jnp.take_along_axis(mirrored[zero_lag // LANES - a - 1], backward, axis=1)
        out_ref[:, a * LANES : (a + 1) * LANES] = jnp.where(lane == 0, high, low)

    span(metas, 1, n - 1, send_m, recv_m.at[0]).wait_send()
    span(plain, 1, n - 1, send_a, recv_a.at[0]).wait_send()
    span(incoming, 0, n - 1, send_b, recv_b).wait_send()


def on_device_slices(spectra, valid, partner, pair_bin, pair_count):
    n = lax.axis_size("chan")
    nchan, nwin, _, nfreq_all = spectra.shape
    nfreq = nfreq_all // n
    nrow = nchan * nwin * 2
    nbins = n * BINS_DEV
    base = 3 * LANES
    deep = n // 2 * LANES
    scale = 1.0 / (math.sqrt(nfreq_all) * nwin * math.sqrt(PAIRS_DEV // BINS_DEV))
    hbm = pl.BlockSpec(memory_space=pltpu.HBM)
    vmem = pl.BlockSpec(memory_space=pltpu.VMEM)
    dma = pltpu.SemaphoreType.DMA
    bf16 = jnp.bfloat16
    return pl.pallas_call(
        functools.partial(kernel, (n, nchan, nwin, nfreq, BINS_DEV)),
        out_shape=pltpu.VMEM((BINS_DEV, LAGS), jnp.float32),
        in_specs=[hbm] * 8,
        out_specs=vmem,
        scratch_shapes=[
            pltpu.VMEM(spectra.shape, bf16),
            pltpu.SMEM(valid.shape, jnp.int32),
            pltpu.SMEM(partner.shape, jnp.int32),
            pltpu.SMEM(pair_bin.shape, jnp.int32),
            pltpu.SMEM(pair_count.shape, jnp.int32),
            pltpu.VMEM((LANES, 6 * LANES), bf16),
            pltpu.VMEM((1, LANES), jnp.int32),
            pltpu.VMEM((n, 1, LANES), jnp.int32),
            pltpu.VMEM((n, nrow, nfreq), bf16),
            pltpu.VMEM((n, nrow, nfreq), bf16),
            pltpu.VMEM((n, nrow, nfreq), bf16),
            pltpu.VMEM((n, nrow, nfreq), bf16),
            pltpu.VMEM((n, nrow, nfreq), bf16),
            pltpu.VMEM((n, nrow, nfreq), bf16),
            pltpu.VMEM((nfreq, 2 * lag_span()), bf16),
            pltpu.VMEM((n, 1, 2 * lag_span()), jnp.float32),
            pltpu.VMEM((n, 8, LANES), jnp.float32),
            pltpu.VMEM((nbins, n // GROUP * base), bf16),
            pltpu.VMEM((nbins, n // GROUP * base), bf16),
            pltpu.VMEM((nbins, deep), bf16),
            pltpu.VMEM((nbins, deep), bf16),
            pltpu.VMEM((2, base, 2 * nfreq), bf16),
            pltpu.VMEM((deep, 2 * nfreq), bf16),
            pltpu.VMEM((nbins, nfreq), jnp.float32),
            pltpu.VMEM((nbins, nfreq), jnp.float32),
            pltpu.VMEM((n, BINS_DEV, 2 * nfreq), bf16),
            pltpu.VMEM((n, BINS_DEV, 2 * nfreq), bf16),
            dma((8,)),
            dma,
            dma((n // GROUP,)),
            dma,
            dma((2,)),
            dma,
            dma,
            pltpu.SemaphoreType.REGULAR,
            pltpu.SemaphoreType.REGULAR,
        ],
        compiler_params=pltpu.CompilerParams(
            collective_id=0, has_side_effects=True, vmem_limit_bytes=60 * 1024 * 1024
        ),
    )(
        spectra,
        valid,
        partner,
        pair_bin,
        pair_count,
        jnp.asarray(expanders(nchan, nwin)),
        jnp.asarray(base_table(nfreq)),
        jnp.asarray(slice_phases(n, nfreq, scale)),
    )


def solution(mesh):
    in_specs = (
        P(("grp", "chan"), None, None, None),
        P(("grp", "chan"), None),
        P(),
        P(("grp", "chan")),
        P(("grp", "chan")),
    )
    out_specs = P(("grp", "chan"), None)
    nblocks = mesh.shape["chan"]
    whole_bands = F % (nblocks * BAND) == 0 and nblocks == GROUP * PLANE
    return jax.shard_map(
        on_device_slices if whole_bands else on_device_blocks,
        mesh=mesh,
        in_specs=in_specs,
        out_specs=out_specs,
        check_vma=False,
    )
```

```python
import functools
import math

import jax
import jax.numpy as jnp
import ml_dtypes
import numpy as np
from jax import lax
from jax.experimental import pallas as pl
from jax.experimental.pallas import tpu as pltpu
from jax.sharding import PartitionSpec as P

F = 4096
BAND = 128
LAGS = 1024
BINS_DEV = 8
PAIRS_DEV = 32
LANES = 128
GROUP = 4
PLANE = 4


def from_partner(block, axis, bit):
    count = lax.axis_size(axis)
    route = []
    for low in range(count):
        high = low | 1 << bit
        if high != low and high < count:
            route += [(low, high), (high, low)]
    return lax.ppermute(block, axis, route)


def whiten(spectra, valid):
    values = spectra.astype(jnp.float32)
    power = values[:, :, 0] * values[:, :, 0] + values[:, :, 1] * values[:, :, 1]
    nchan, nwin, nfreq = power.shape
    banded = jnp.mean(power.reshape(nchan, nwin, nfreq // BAND, BAND), axis=-1)
    amplitude = jnp.repeat(jnp.sqrt(banded + 1e-06), BAND, axis=-1)
    weights = valid.astype(jnp.float32)[:, :, None, None]
    return (values * weights / amplitude[:, :, None, :]).astype(jnp.bfloat16)


def lag_table():
    freqs = jnp.arange(F, dtype=jnp.int32)
    shifts = jnp.arange(LAGS, dtype=jnp.int32) - LAGS // 2
    phase = jnp.mod(freqs[:, None] * shifts[None, :], 2 * F)
    angle = phase.astype(jnp.float32) * (2.0 * math.pi / (2 * F))
    scale = 1.0 / math.sqrt(F)
    return jnp.concatenate([jnp.cos(angle) * scale, -jnp.sin(angle) * scale], axis=0).astype(
        jnp.bfloat16
    )


def cross_product(left_part, right_part):
    return jnp.einsum("awf,bwf->abf", left_part, right_part, preferred_element_type=jnp.float32)


def correlate(own_block, other_block, table):
    own_real = own_block[:, :, 0]
    own_imag = own_block[:, :, 1]
    oth_real = other_block[:, :, 0]
    oth_imag = other_block[:, :, 1]
    real_part = cross_product(own_real, oth_real) + cross_product(own_imag, oth_imag)
    imag_part = cross_product(own_imag, oth_real) - cross_product(own_real, oth_imag)
    nchan = own_block.shape[0]
    nwin = own_block.shape[1]
    spec = (jnp.concatenate([real_part, imag_part], axis=-1) * (1.0 / nwin)).reshape(
        nchan * nchan, -1
    )
    spec = spec.astype(jnp.bfloat16)
    return jnp.dot(spec, table, preferred_element_type=jnp.float32)


def select_sum(selector, corr_high, corr_low):
    return jnp.dot(selector, corr_high, preferred_element_type=jnp.float32) + jnp.dot(
        selector, corr_low, preferred_element_type=jnp.float32
    )


def on_device_blocks(spectra, valid, partner, pair_bin, pair_count):
    white = whiten(spectra, valid)
    nblocks = lax.axis_size("chan")
    round_mask = partner[0]
    paired = white
    for bit_index in range(nblocks.bit_length() - 1):
        swapped = from_partner(paired, "chan", bit_index)
        paired = jnp.where(round_mask >> bit_index & 1 == 1, swapped, paired)
    table = lag_table()
    self_corr = correlate(white, white, table)
    cross_corr = correlate(white, paired, table)
    corr = jnp.concatenate([self_corr, cross_corr], axis=0)
    corr_high = corr.astype(jnp.bfloat16)
    corr_low = (corr - corr_high.astype(jnp.float32)).astype(jnp.bfloat16)
    rows = jnp.arange(corr.shape[0], dtype=jnp.int32)
    live_rows = (rows < pair_count[0]) & (pair_bin >= 0)
    kept_bins = jnp.where(live_rows, pair_bin, -1)
    targets = lax.iota(jnp.int32, nblocks * BINS_DEV)
    selector = (kept_bins[None, :] == targets[:, None]).astype(jnp.bfloat16)
    terms = select_sum(selector, corr_high, corr_low).reshape(nblocks, BINS_DEV, -1)
    received = lax.all_to_all(terms, "chan", split_axis=0, concat_axis=0, tiled=True)
    summed = jnp.sum(received, axis=0)
    return summed * (1.0 / math.sqrt(PAIRS_DEV // BINS_DEV))


def lag_span():
    return LAGS // 2 + LANES


def interleaved(cos, sin):
    tiled = [part.reshape(part.shape[0], -1, 1, LANES) for part in (cos, sin)]
    return np.concatenate(tiled, axis=2).reshape(cos.shape[0], -1)


def base_table(nfreq):
    shifts = np.arange(lag_span())
    angle = np.mod(np.arange(nfreq)[:, None] * shifts[None, :], 2 * F) * (2.0 * math.pi / (2 * F))
    return interleaved(np.cos(angle), np.sin(angle)).astype(ml_dtypes.bfloat16)


def slice_phases(nslices, nfreq, scale):
    shifts = np.arange(lag_span())
    first = np.arange(nslices) * nfreq
    angle = np.mod(first[:, None] * shifts[None, :], 2 * F) * (2.0 * math.pi / (2 * F))
    both = interleaved(np.cos(angle), np.sin(angle)) * scale
    return both.astype(np.float32)[:, None, :]


def expanders(nchan, nwin):
    row = np.arange(LANES)
    per_chan = 2 * nwin
    chan = row // per_chan % nchan
    shift = row // (per_chan * nchan)
    npairs = nchan * nchan

    def pair(step):
        return chan * nchan + (chan + step) % nchan

    def reverse(step):
        return (chan + step) % nchan * nchan + chan

    lanes = (
        pair(0),
        pair(1),
        reverse(1),
        pair(2),
        npairs + pair(shift),
        npairs + reverse(shift),
    )
    return np.concatenate(
        [(np.arange(LANES)[:, None] == lane[None, :]) for lane in lanes], axis=1
    ).astype(ml_dtypes.bfloat16)


def swap_pairs(rows):
    size = rows.shape[-2]
    axis = rows.ndim - 2
    even = lax.broadcasted_iota(jnp.int32, rows.shape, axis) % 2 == 0
    return jnp.where(
        even, pltpu.roll(rows, size - 1, axis), pltpu.roll(rows, 1, axis)
    ), even


def halves_swapped(rows):
    half = rows.shape[0] // 2
    return jnp.concatenate([rows[half:], rows[:half]], axis=0)


def kernel(
    dims,
    spectra_hbm,
    valid_hbm,
    partner_hbm,
    bin_hbm,
    count_hbm,
    expand_hbm,
    table_hbm,
    phase_hbm,
    out_ref,
    own,
    valid_ref,
    partner_ref,
    bin_ref,
    count_ref,
    expand_ref,
    meta_ref,
    metas,
    white,
    plain,
    same,
    odd,
    plain_turn,
    odd_turn,
    table,
    phases,
    cross_bins,
    select_re,
    select_im,
    cross_re,
    cross_im,
    products,
    cross_products,
    total_re,
    total_im,
    outgoing,
    incoming,
    local_sems,
    send_a,
    recv_a,
    send_m,
    recv_m,
    send_b,
    recv_b,
    ready,
    token,
):
    n, nchan, nwin, nfreq, nbins_dev = dims
    nrow = nchan * nwin * 2
    nbins = n * nbins_dev
    npairs = nchan * nchan
    ngroups = n // GROUP
    half = n // 2
    me = lax.axis_index("chan")

    def peer(k):
        bits = range((n - 1).bit_length())
        return sum((me // 2**b + k // 2**b) % 2 * 2**b for b in bits)

    def remote(src, dst, send, recv, target):
        return pltpu.make_async_remote_copy(
            src_ref=src,
            dst_ref=dst,
            send_sem=send,
            recv_sem=recv,
            device_id={"chan": target},
            device_id_type=pl.DeviceIdType.MESH,
        )

    def span(buffer, first, count, send, recv):
        part = buffer.at[pl.ds(first, count)]
        return remote(part, part, send, recv, peer(1))

    copy_own = pltpu.make_async_copy(spectra_hbm, own, local_sems.at[0])
    copy_table = pltpu.make_async_copy(table_hbm, table, local_sems.at[1])
    copy_phase = pltpu.make_async_copy(phase_hbm, phases, local_sems.at[2])
    small = [
        pltpu.make_async_copy(src, dst, local_sems.at[3 + i])
        for i, (src, dst) in enumerate(
            (
                (valid_hbm, valid_ref),
                (bin_hbm, bin_ref),
                (count_hbm, count_ref),
                (partner_hbm, partner_ref),
                (expand_hbm, expand_ref),
            )
        )
    ]
    plane = me // PLANE
    is_last = plane == n // PLANE - 1
    barrier = pltpu.get_barrier_semaphore()

    def signal(sem, ks):
        for k in ks:
            pl.semaphore_signal(
                sem,
                inc=1,
                device_id={"chan": peer(k)},
                device_id_type=pl.DeviceIdType.MESH,
            )

    @pl.when(jnp.logical_not(is_last))
    def _():
        signal(barrier, range(n - 1, 0, -1))

    copy_own.start()
    for copy in small:
        copy.start()
    copy_table.start()
    copy_phase.start()
    for copy in small[:3]:
        copy.wait()

    lane = lax.broadcasted_iota(jnp.int32, meta_ref.shape, 1)
    bins = jnp.full(meta_ref.shape, -1, jnp.int32)
    for row in range(2 * npairs):
        bins = jnp.where(lane == row, bin_ref[row], bins)
    bins = jnp.where((lane < count_ref[0]) & (bins >= 0), bins, -1)
    meta_ref[...] = bins

    sub = lax.broadcasted_iota(jnp.int32, (nchan, 2 * nwin, LANES), 1) // 2
    chan = lax.broadcasted_iota(jnp.int32, (nchan, 2 * nwin, LANES), 0)
    usable = jnp.zeros((nchan, 2 * nwin, LANES), jnp.float32)
    for c in range(nchan):
        for w in range(nwin):
            usable = jnp.where(
                (chan == c) & (sub == w), valid_ref[c, w].astype(jnp.float32), usable
            )

    def whiten_slice(t):
        here = pl.ds(pl.multiple_of(t * nfreq, nfreq), nfreq)
        x = own[:, :, :, here].astype(jnp.float32)
        x = x.reshape(nchan, 2 * nwin, nfreq)
        swapped, _ = swap_pairs(x)
        power = x * x + swapped * swapped
        for b in range(nfreq // BAND):
            band = slice(b * BAND, (b + 1) * BAND)
            total = jnp.sum(power[:, :, band], axis=-1, keepdims=True)
            scale = lax.rsqrt(total * (1.0 / BAND) + 1e-06) * usable
            rows = (x[:, :, band] * scale).reshape(nrow, BAND)
            white[t, :, band] = rows.astype(jnp.bfloat16)

    def send_meta(k):
        remote(meta_ref, metas.at[k], send_m, recv_m.at[k // half], peer(k)).start()

    def send_white(k):
        remote(white.at[peer(k)], plain.at[k], send_a, recv_a.at[k // GROUP], peer(k)).start()

    def each(act, ks):
        for k in ks:
            act(k)

    near = [7, 6, 5, 4]
    middle = [11, 10, 9, 8]
    far = [15, 14, 13, 12]
    inside = [3, 2, 1]
    copy_own.wait()

    @pl.when(jnp.logical_not(is_last))
    def _():
        def step(i, carry):
            for u in range(4):
                whiten_slice(4 * i + u)
            return carry

        lax.fori_loop(0, n // 4, step, 0)
        pl.semaphore_wait(barrier, 3 * PLANE - 1)

    @pl.when(is_last)
    def _():
        pl.semaphore_wait(barrier, 3 * PLANE)
        signal(ready, far + middle + near)
        each(send_meta, far + middle + near)
        for k in far + middle + near:
            whiten_slice(peer(k))
            send_white(k)
        for k in [*inside, 0]:
            whiten_slice(peer(k))
        pl.semaphore_wait(token, 1)
        each(send_meta, inside)
        each(send_white, inside)

    @pl.when(plane == 2)
    def _():
        each(send_meta, far + middle + inside)
        each(send_white, far + middle)
        pl.semaphore_wait(ready, PLANE)
        signal(token, near[-1:])
        each(send_meta, near)
        each(send_white, near + inside)

    @pl.when(plane == 1)
    def _():
        each(send_meta, far + near + inside)
        each(send_white, far + near)
        pl.semaphore_wait(ready, PLANE)
        each(send_meta, middle)
        each(send_white, middle + inside)

    @pl.when(plane == 0)
    def _():
        each(send_meta, middle + near + inside)
        each(send_white, middle)
        pl.semaphore_wait(ready, PLANE)
        each(send_meta, far)
        each(send_white, far + near + inside)

    plain[0] = white[me]
    metas[0] = meta_ref[...]
    for copy in small[3:]:
        copy.wait()
    mirror = partner_ref[0]
    across = mirror // PLANE
    lead = jnp.where(across == 2, 1, 0)
    early, late = [], []
    for j in range(PLANE):
        inner = jnp.where(mirror == 2, j % 2, j % 2 * 2)
        early.append(jnp.where(across == 0, j // 2 * PLANE + inner, lead * PLANE + j))
        late.append(jnp.where(across == 0, (3 - j // 2) * PLANE + inner, 2 * PLANE + j))
    firsts = early + late
    sequence = [0, 1, 3, 2]

    def prepare(k):
        same[k] = plain[k]
        x = plain[k].astype(jnp.float32)
        swapped, even = swap_pairs(x)
        turn = jnp.where(even, -swapped, swapped)
        step = 2 * nwin
        odd[k] = jnp.concatenate([x[step:], x[:step]], axis=0).astype(jnp.bfloat16)
        plain_turn[k] = turn.astype(jnp.bfloat16)
        odd_turn[k] = jnp.concatenate([turn[step:], turn[:step]], axis=0).astype(jnp.bfloat16)

    def put(target, at, left, right, right_turn):
        target[pl.ds(at, nrow), 0:nfreq] = left * right
        target[pl.ds(at, nrow), nfreq : 2 * nfreq] = left * right_turn

    def multiply_self(target, g):
        for u in range(GROUP):
            k = g * GROUP + u
            x = plain[k]
            xt = plain_turn[k]
            put(target, u * nrow, x, x, xt)
            put(target, LANES + u * nrow, x, odd[k], odd_turn[k])
            put(target, 2 * LANES + u * nrow, x, halves_swapped(x), halves_swapped(xt))

    base = 3 * LANES

    bin_rows = lax.broadcasted_iota(jnp.int32, (nbins, LANES), 0)
    bin_rows = bin_rows.astype(jnp.float32).astype(jnp.bfloat16)
    one = jnp.ones((nbins, LANES), jnp.bfloat16)
    zero = jnp.zeros((nbins, LANES), jnp.bfloat16)

    def one_hot(row):
        return jnp.where(bin_rows == row.astype(jnp.bfloat16), one, zero)

    def select_self(part):
        first = part * half
        count = half - (part == 0)
        span(metas, first + (part == 0), count, send_m, recv_m.at[part]).wait_recv()
        spread = jnp.dot(
            metas[first : first + half, 0, :].astype(jnp.float32).astype(jnp.bfloat16),
            expand_ref[...],
            preferred_element_type=jnp.float32,
        )
        for u in range(half):
            cross_bins[first + u, 0:1, :] = spread[u : u + 1, 4 * LANES : 5 * LANES]
            cross_bins[first + u, 1:2, :] = spread[u : u + 1, 5 * LANES : 6 * LANES]
        self_bins = spread[:, : 4 * LANES]
        slot = lax.broadcasted_iota(jnp.int32, self_bins.shape, 0) % GROUP
        place = lax.broadcasted_iota(jnp.int32, self_bins.shape, 1) % LANES // nrow
        self_bins = jnp.where(slot == place, self_bins, 0.0)
        for v in range(half // GROUP):
            i = sequence.index(part * half // GROUP + v)
            row = jnp.sum(self_bins[v * GROUP : (v + 1) * GROUP], axis=0, keepdims=True)
            alone, ahead, back, over = [
                one_hot(row[:, h * LANES : (h + 1) * LANES]) for h in range(4)
            ]
            at = i * base
            for target, mixed in ((select_re, ahead + back), (select_im, ahead - back)):
                target[:, at : at + LANES] = alone
                target[:, at + LANES : at + 2 * LANES] = mixed
                target[:, at + 2 * LANES : at + 3 * LANES] = over

    def select_cross():
        for j in range(n // 2):
            ahead = one_hot(cross_bins[firsts[j], 0:1, :])
            back = one_hot(cross_bins[firsts[j] ^ mirror, 1:2, :])
            cross_re[:, j * LANES : (j + 1) * LANES] = ahead + back
            cross_im[:, j * LANES : (j + 1) * LANES] = ahead - back

    def product(left, right):
        return jnp.dot(left, right, preferred_element_type=jnp.float32)

    def multiply_cross(j):
        x = same[firsts[j]]
        q = firsts[j] ^ mirror
        at = j * LANES
        y, yt, z, zt = same[q], plain_turn[q], odd[q], odd_turn[q]
        put(cross_products, at, x, y, yt)
        put(cross_products, at + nrow, x, z, zt)
        put(cross_products, at + 2 * nrow, x, halves_swapped(y), halves_swapped(yt))
        put(cross_products, at + 3 * nrow, x, halves_swapped(z), halves_swapped(zt))

    def cross_sum(selector, first, last, columns):
        rows = slice(first * LANES, last * LANES)
        return product(selector[:, rows], cross_products[rows, columns])

    def self_sum(selector, i, columns):
        return product(selector[:, i * base : (i + 1) * base], products[i % 2, :, columns])

    real, imag = slice(0, nfreq), slice(nfreq, 2 * nfreq)
    def collect(i):
        g = sequence[i]
        here = range(max(g * GROUP, 1), (g + 1) * GROUP)
        span(plain, here[0], len(here), send_a, recv_a.at[g]).wait_recv()
        for k in range(g * GROUP, (g + 1) * GROUP):
            prepare(k)
        multiply_self(products.at[i % 2], g)

    collect(0)
    collect(1)
    select_self(0)
    total_re[...] = self_sum(select_re, 0, real) + self_sum(select_re, 1, real)
    total_im[...] = self_sum(select_im, 0, imag) + self_sum(select_im, 1, imag)
    select_self(1)
    select_cross()
    collect(2)
    for j in range(PLANE):
        multiply_cross(j)
    total_re[...] += self_sum(select_re, 2, real) + cross_sum(cross_re, 0, PLANE, real)
    total_im[...] += self_sum(select_im, 2, imag) + cross_sum(cross_im, 0, PLANE, imag)
    collect(3)
    for j in range(PLANE, 2 * PLANE):
        multiply_cross(j)
    last = ngroups - 1
    terms_re = (
        total_re[...]
        + self_sum(select_re, last, real)
        + cross_sum(cross_re, PLANE, 2 * PLANE, real)
    )
    terms_re = terms_re.reshape(n, nbins_dev, nfreq).astype(jnp.bfloat16)
    terms_im = (
        total_im[...]
        + self_sum(select_im, last, imag)
        + cross_sum(cross_im, PLANE, 2 * PLANE, imag)
    )
    terms_im = terms_im.reshape(n, nbins_dev, nfreq).astype(jnp.bfloat16)
    outgoing[:, :, real] = terms_re
    outgoing[:, :, imag] = terms_im

    for i in range(n - 1):
        target = i + (i + n - me) // n
        remote(outgoing.at[target], incoming.at[me], send_b, recv_b, target).start()
    incoming[me] = outgoing[me]
    copy_table.wait()
    copy_phase.wait()
    span(incoming, 0, n - 1, send_b, recv_b).wait_recv()

    arrived = incoming[...].astype(jnp.float32).reshape(nbins, 2 * nfreq).astype(jnp.bfloat16)
    stacked = jnp.concatenate([arrived[:, real], arrived[:, imag]], axis=0)
    zero_lag = LAGS // 2
    lane = lax.broadcasted_iota(jnp.int32, (nbins_dev, LANES), 1)
    backward = (LANES - lane) % LANES
    mirrored = []
    for a in range(lag_span() // LANES):
        both = slice(2 * a * LANES, 2 * (a + 1) * LANES)
        lags = product(stacked, table[:, both]).reshape(2, n, nbins_dev, 2 * LANES)
        cos, sin = phases[:, :, both][:, :, :LANES], phases[:, :, both][:, :, LANES:]
        even_part = jnp.sum(lags[0, :, :, :LANES] * cos - lags[0, :, :, LANES:] * sin, axis=0)
        odd_part = jnp.sum(lags[1, :, :, LANES:] * cos + lags[1, :, :, :LANES] * sin, axis=0)
        if a < zero_lag // LANES:
            out_ref[:, zero_lag + a * LANES : zero_lag + (a + 1) * LANES] = even_part - odd_part
        mirrored.append(even_part + odd_part)
    for a in range(zero_lag // LANES):
        high = mirrored[zero_lag // LANES - a]
        low = jnp.take_along_axis(mirrored[zero_lag // LANES - a - 1], backward, axis=1)
        out_ref[:, a * LANES : (a + 1) * LANES] = jnp.where(lane == 0, high, low)

    span(metas, 1, n - 1, send_m, recv_m.at[0]).wait_send()
    span(plain, 1, n - 1, send_a, recv_a.at[0]).wait_send()
    span(incoming, 0, n - 1, send_b, recv_b).wait_send()


def on_device_slices(spectra, valid, partner, pair_bin, pair_count):
    n = lax.axis_size("chan")
    nchan, nwin, _, nfreq_all = spectra.shape
    nfreq = nfreq_all // n
    nrow = nchan * nwin * 2
    nbins = n * BINS_DEV
    base = 3 * LANES
    deep = n // 2 * LANES
    scale = 1.0 / (math.sqrt(nfreq_all) * nwin * math.sqrt(PAIRS_DEV // BINS_DEV))
    hbm = pl.BlockSpec(memory_space=pltpu.HBM)
    vmem = pl.BlockSpec(memory_space=pltpu.VMEM)
    dma = pltpu.SemaphoreType.DMA
    bf16 = jnp.bfloat16
    return pl.pallas_call(
        functools.partial(kernel, (n, nchan, nwin, nfreq, BINS_DEV)),
        out_shape=pltpu.VMEM((BINS_DEV, LAGS), jnp.float32),
        in_specs=[hbm] * 8,
        out_specs=vmem,
        scratch_shapes=[
            pltpu.VMEM(spectra.shape, bf16),
            pltpu.SMEM(valid.shape, jnp.int32),
            pltpu.SMEM(partner.shape, jnp.int32),
            pltpu.SMEM(pair_bin.shape, jnp.int32),
            pltpu.SMEM(pair_count.shape, jnp.int32),
            pltpu.VMEM((LANES, 6 * LANES), bf16),
            pltpu.VMEM((1, LANES), jnp.int32),
            pltpu.VMEM((n, 1, LANES), jnp.int32),
            pltpu.VMEM((n, nrow, nfreq), bf16),
            pltpu.VMEM((n, nrow, nfreq), bf16),
            pltpu.VMEM((n, nrow, nfreq), bf16),
            pltpu.VMEM((n, nrow, nfreq), bf16),
            pltpu.VMEM((n, nrow, nfreq), bf16),
            pltpu.VMEM((n, nrow, nfreq), bf16),
            pltpu.VMEM((nfreq, 2 * lag_span()), bf16),
            pltpu.VMEM((n, 1, 2 * lag_span()), jnp.float32),
            pltpu.VMEM((n, 8, LANES), jnp.float32),
            pltpu.VMEM((nbins, n // GROUP * base), bf16),
            pltpu.VMEM((nbins, n // GROUP * base), bf16),
            pltpu.VMEM((nbins, deep), bf16),
            pltpu.VMEM((nbins, deep), bf16),
            pltpu.VMEM((2, base, 2 * nfreq), bf16),
            pltpu.VMEM((deep, 2 * nfreq), bf16),
            pltpu.VMEM((nbins, nfreq), jnp.float32),
            pltpu.VMEM((nbins, nfreq), jnp.float32),
            pltpu.VMEM((n, BINS_DEV, 2 * nfreq), bf16),
            pltpu.VMEM((n, BINS_DEV, 2 * nfreq), bf16),
            dma((8,)),
            dma,
            dma((n // GROUP,)),
            dma,
            dma((2,)),
            dma,
            dma,
            pltpu.SemaphoreType.REGULAR,
            pltpu.SemaphoreType.REGULAR,
        ],
        compiler_params=pltpu.CompilerParams(
            collective_id=0, has_side_effects=True, vmem_limit_bytes=60 * 1024 * 1024
        ),
    )(
        spectra,
        valid,
        partner,
        pair_bin,
        pair_count,
        jnp.asarray(expanders(nchan, nwin)),
        jnp.asarray(base_table(nfreq)),
        jnp.asarray(slice_phases(n, nfreq, scale)),
    )


def solution(mesh):
    in_specs = (
        P(("grp", "chan"), None, None, None),
        P(("grp", "chan"), None),
        P(),
        P(("grp", "chan")),
        P(("grp", "chan")),
    )
    out_specs = P(("grp", "chan"), None)
    nblocks = mesh.shape["chan"]
    whole_bands = F % (nblocks * BAND) == 0 and nblocks == GROUP * PLANE
    return jax.shard_map(
        on_device_slices if whole_bands else on_device_blocks,
        mesh=mesh,
        in_specs=in_specs,
        out_specs=out_specs,
        check_vma=False,
    )
```

```python
import functools
import math

import jax
import jax.numpy as jnp
import ml_dtypes
import numpy as np
from jax import lax
from jax.experimental import pallas as pl
from jax.experimental.pallas import tpu as pltpu
from jax.sharding import PartitionSpec as P

F = 4096
BAND = 128
LAGS = 1024
BINS_DEV = 8
PAIRS_DEV = 32
LANES = 128
GROUP = 4
PLANE = 4


def from_partner(block, axis, bit):
    count = lax.axis_size(axis)
    route = []
    for low in range(count):
        high = low | 1 << bit
        if high != low and high < count:
            route += [(low, high), (high, low)]
    return lax.ppermute(block, axis, route)


def whiten(spectra, valid):
    values = spectra.astype(jnp.float32)
    power = values[:, :, 0] * values[:, :, 0] + values[:, :, 1] * values[:, :, 1]
    nchan, nwin, nfreq = power.shape
    banded = jnp.mean(power.reshape(nchan, nwin, nfreq // BAND, BAND), axis=-1)
    amplitude = jnp.repeat(jnp.sqrt(banded + 1e-06), BAND, axis=-1)
    weights = valid.astype(jnp.float32)[:, :, None, None]
    return (values * weights / amplitude[:, :, None, :]).astype(jnp.bfloat16)


def lag_table():
    freqs = jnp.arange(F, dtype=jnp.int32)
    shifts = jnp.arange(LAGS, dtype=jnp.int32) - LAGS // 2
    phase = jnp.mod(freqs[:, None] * shifts[None, :], 2 * F)
    angle = phase.astype(jnp.float32) * (2.0 * math.pi / (2 * F))
    scale = 1.0 / math.sqrt(F)
    return jnp.concatenate([jnp.cos(angle) * scale, -jnp.sin(angle) * scale], axis=0).astype(
        jnp.bfloat16
    )


def cross_product(left_part, right_part):
    return jnp.einsum("awf,bwf->abf", left_part, right_part, preferred_element_type=jnp.float32)


def correlate(own_block, other_block, table):
    own_real = own_block[:, :, 0]
    own_imag = own_block[:, :, 1]
    oth_real = other_block[:, :, 0]
    oth_imag = other_block[:, :, 1]
    real_part = cross_product(own_real, oth_real) + cross_product(own_imag, oth_imag)
    imag_part = cross_product(own_imag, oth_real) - cross_product(own_real, oth_imag)
    nchan = own_block.shape[0]
    nwin = own_block.shape[1]
    spec = (jnp.concatenate([real_part, imag_part], axis=-1) * (1.0 / nwin)).reshape(
        nchan * nchan, -1
    )
    spec = spec.astype(jnp.bfloat16)
    return jnp.dot(spec, table, preferred_element_type=jnp.float32)


def select_sum(selector, corr_high, corr_low):
    return jnp.dot(selector, corr_high, preferred_element_type=jnp.float32) + jnp.dot(
        selector, corr_low, preferred_element_type=jnp.float32
    )


def on_device_blocks(spectra, valid, partner, pair_bin, pair_count):
    white = whiten(spectra, valid)
    nblocks = lax.axis_size("chan")
    round_mask = partner[0]
    paired = white
    for bit_index in range(nblocks.bit_length() - 1):
        swapped = from_partner(paired, "chan", bit_index)
        paired = jnp.where(round_mask >> bit_index & 1 == 1, swapped, paired)
    table = lag_table()
    self_corr = correlate(white, white, table)
    cross_corr = correlate(white, paired, table)
    corr = jnp.concatenate([self_corr, cross_corr], axis=0)
    corr_high = corr.astype(jnp.bfloat16)
    corr_low = (corr - corr_high.astype(jnp.float32)).astype(jnp.bfloat16)
    rows = jnp.arange(corr.shape[0], dtype=jnp.int32)
    live_rows = (rows < pair_count[0]) & (pair_bin >= 0)
    kept_bins = jnp.where(live_rows, pair_bin, -1)
    targets = lax.iota(jnp.int32, nblocks * BINS_DEV)
    selector = (kept_bins[None, :] == targets[:, None]).astype(jnp.bfloat16)
    terms = select_sum(selector, corr_high, corr_low).reshape(nblocks, BINS_DEV, -1)
    received = lax.all_to_all(terms, "chan", split_axis=0, concat_axis=0, tiled=True)
    summed = jnp.sum(received, axis=0)
    return summed * (1.0 / math.sqrt(PAIRS_DEV // BINS_DEV))


def lag_span():
    return LAGS // 2 + LANES


def interleaved(cos, sin):
    tiled = [part.reshape(part.shape[0], -1, 1, LANES) for part in (cos, sin)]
    return np.concatenate(tiled, axis=2).reshape(cos.shape[0], -1)


def base_table(nfreq):
    shifts = np.arange(lag_span())
    angle = np.mod(np.arange(nfreq)[:, None] * shifts[None, :], 2 * F) * (2.0 * math.pi / (2 * F))
    return interleaved(np.cos(angle), np.sin(angle)).astype(ml_dtypes.bfloat16)


def slice_phases(nslices, nfreq, scale):
    shifts = np.arange(lag_span())
    first = np.arange(nslices) * nfreq
    angle = np.mod(first[:, None] * shifts[None, :], 2 * F) * (2.0 * math.pi / (2 * F))
    both = interleaved(np.cos(angle), np.sin(angle)) * scale
    return both.astype(np.float32)[:, None, :]


def expanders(nchan, nwin):
    row = np.arange(LANES)
    per_chan = 2 * nwin
    chan = row // per_chan % nchan
    shift = row // (per_chan * nchan)
    npairs = nchan * nchan

    def pair(step):
        return chan * nchan + (chan + step) % nchan

    def reverse(step):
        return (chan + step) % nchan * nchan + chan

    lanes = (
        pair(0),
        pair(1),
        reverse(1),
        pair(2),
        npairs + pair(shift),
        npairs + reverse(shift),
    )
    return np.concatenate(
        [(np.arange(LANES)[:, None] == lane[None, :]) for lane in lanes], axis=1
    ).astype(ml_dtypes.bfloat16)


def swap_pairs(rows):
    size = rows.shape[-2]
    axis = rows.ndim - 2
    even = lax.broadcasted_iota(jnp.int32, rows.shape, axis) % 2 == 0
    return jnp.where(
        even, pltpu.roll(rows, size - 1, axis), pltpu.roll(rows, 1, axis)
    ), even


def halves_swapped(rows):
    half = rows.shape[0] // 2
    return jnp.concatenate([rows[half:], rows[:half]], axis=0)


def kernel(
    dims,
    spectra_hbm,
    valid_hbm,
    partner_hbm,
    bin_hbm,
    count_hbm,
    expand_hbm,
    table_hbm,
    phase_hbm,
    out_ref,
    own,
    valid_ref,
    partner_ref,
    bin_ref,
    count_ref,
    expand_ref,
    meta_ref,
    metas,
    white,
    plain,
    same,
    odd,
    plain_turn,
    odd_turn,
    table,
    phases,
    cross_bins,
    select_re,
    select_im,
    cross_re,
    cross_im,
    products,
    cross_products,
    total_re,
    total_im,
    outgoing,
    incoming,
    local_sems,
    send_a,
    recv_a,
    send_m,
    recv_m,
    send_b,
    recv_b,
    ready,
    token,
):
    n, nchan, nwin, nfreq, nbins_dev = dims
    nrow = nchan * nwin * 2
    nbins = n * nbins_dev
    npairs = nchan * nchan
    ngroups = n // GROUP
    half = n // 2
    me = lax.axis_index("chan")

    def peer(k):
        bits = range((n - 1).bit_length())
        return sum((me // 2**b + k // 2**b) % 2 * 2**b for b in bits)

    def remote(src, dst, send, recv, target):
        return pltpu.make_async_remote_copy(
            src_ref=src,
            dst_ref=dst,
            send_sem=send,
            recv_sem=recv,
            device_id={"chan": target},
            device_id_type=pl.DeviceIdType.MESH,
        )

    def span(buffer, first, count, send, recv):
        part = buffer.at[pl.ds(first, count)]
        return remote(part, part, send, recv, peer(1))

    copy_own = pltpu.make_async_copy(spectra_hbm, own, local_sems.at[0])
    copy_table = pltpu.make_async_copy(table_hbm, table, local_sems.at[1])
    copy_phase = pltpu.make_async_copy(phase_hbm, phases, local_sems.at[2])
    small = [
        pltpu.make_async_copy(src, dst, local_sems.at[3 + i])
        for i, (src, dst) in enumerate(
            (
                (valid_hbm, valid_ref),
                (bin_hbm, bin_ref),
                (count_hbm, count_ref),
                (partner_hbm, partner_ref),
                (expand_hbm, expand_ref),
            )
        )
    ]
    plane = me // PLANE
    is_last = plane == n // PLANE - 1
    barrier = pltpu.get_barrier_semaphore()

    def signal(sem, ks):
        for k in ks:
            pl.semaphore_signal(
                sem,
                inc=1,
                device_id={"chan": peer(k)},
                device_id_type=pl.DeviceIdType.MESH,
            )

    @pl.when(jnp.logical_not(is_last))
    def _():
        signal(barrier, range(n - 1, 0, -1))

    copy_own.start()
    for copy in small:
        copy.start()
    copy_table.start()
    copy_phase.start()
    near = [7, 6, 5, 4]
    middle = [11, 10, 9, 8]
    far = [15, 14, 13, 12]
    inside = [3, 2, 1]

    @pl.when(is_last)
    def _():
        pl.semaphore_wait(barrier, 3 * PLANE)
        signal(ready, far + middle + near)

    for copy in small[:3]:
        copy.wait()

    lane = lax.broadcasted_iota(jnp.int32, meta_ref.shape, 1)
    bins = jnp.full(meta_ref.shape, -1, jnp.int32)
    for row in range(2 * npairs):
        bins = jnp.where(lane == row, bin_ref[row], bins)
    bins = jnp.where((lane < count_ref[0]) & (bins >= 0), bins, -1)
    meta_ref[...] = bins

    sub = lax.broadcasted_iota(jnp.int32, (nchan, 2 * nwin, LANES), 1) // 2
    chan = lax.broadcasted_iota(jnp.int32, (nchan, 2 * nwin, LANES), 0)
    usable = jnp.zeros((nchan, 2 * nwin, LANES), jnp.float32)
    for c in range(nchan):
        for w in range(nwin):
            usable = jnp.where(
                (chan == c) & (sub == w), valid_ref[c, w].astype(jnp.float32), usable
            )

    def whiten_slice(t):
        here = pl.ds(pl.multiple_of(t * nfreq, nfreq), nfreq)
        x = own[:, :, :, here].astype(jnp.float32)
        x = x.reshape(nchan, 2 * nwin, nfreq)
        swapped, _ = swap_pairs(x)
        power = x * x + swapped * swapped
        for b in range(nfreq // BAND):
            band = slice(b * BAND, (b + 1) * BAND)
            total = jnp.sum(power[:, :, band], axis=-1, keepdims=True)
            scale = lax.rsqrt(total * (1.0 / BAND) + 1e-06) * usable
            rows = (x[:, :, band] * scale).reshape(nrow, BAND)
            white[t, :, band] = rows.astype(jnp.bfloat16)

    def send_meta(k):
        remote(meta_ref, metas.at[k], send_m, recv_m.at[k // half], peer(k)).start()

    def send_white(k):
        remote(white.at[peer(k)], plain.at[k], send_a, recv_a.at[k // GROUP], peer(k)).start()

    def each(act, ks):
        for k in ks:
            act(k)

    copy_own.wait()

    @pl.when(jnp.logical_not(is_last))
    def _():
        def step(i, carry):
            for u in range(4):
                whiten_slice(4 * i + u)
            return carry

        lax.fori_loop(0, n // 4, step, 0)
        pl.semaphore_wait(barrier, 3 * PLANE - 1)

    @pl.when(is_last)
    def _():
        each(send_meta, far + middle + near)
        for k in far + middle + near:
            whiten_slice(peer(k))
            send_white(k)
        for k in [*inside, 0]:
            whiten_slice(peer(k))
        pl.semaphore_wait(token, 1)
        each(send_meta, inside)
        each(send_white, inside)

    @pl.when(plane == 2)
    def _():
        each(send_meta, far + middle + inside)
        each(send_white, far + middle)
        pl.semaphore_wait(ready, PLANE)
        signal(token, near[-1:])
        each(send_meta, near)
        each(send_white, near + inside)

    @pl.when(plane == 1)
    def _():
        each(send_meta, far + near + inside)
        each(send_white, far + near)
        pl.semaphore_wait(ready, PLANE)
        each(send_meta, middle)
        each(send_white, middle + inside)

    @pl.when(plane == 0)
    def _():
        each(send_meta, middle + near + inside)
        each(send_white, middle)
        pl.semaphore_wait(ready, PLANE)
        each(send_meta, far)
        each(send_white, far + near + inside)

    plain[0] = white[me]
    metas[0] = meta_ref[...]
    for copy in small[3:]:
        copy.wait()
    mirror = partner_ref[0]
    across = mirror // PLANE
    lead = jnp.where(across == 2, 1, 0)
    early, late = [], []
    for j in range(PLANE):
        inner = jnp.where(mirror == 2, j % 2, j % 2 * 2)
        early.append(jnp.where(across == 0, j // 2 * PLANE + inner, lead * PLANE + j))
        late.append(jnp.where(across == 0, (3 - j // 2) * PLANE + inner, 2 * PLANE + j))
    firsts = early + late
    sequence = [0, 1, 3, 2]

    def prepare(k):
        same[k] = plain[k]
        x = plain[k].astype(jnp.float32)
        swapped, even = swap_pairs(x)
        turn = jnp.where(even, -swapped, swapped)
        step = 2 * nwin
        odd[k] = jnp.concatenate([x[step:], x[:step]], axis=0).astype(jnp.bfloat16)
        plain_turn[k] = turn.astype(jnp.bfloat16)
        odd_turn[k] = jnp.concatenate([turn[step:], turn[:step]], axis=0).astype(jnp.bfloat16)

    def put(target, at, left, right, right_turn):
        target[pl.ds(at, nrow), 0:nfreq] = left * right
        target[pl.ds(at, nrow), nfreq : 2 * nfreq] = left * right_turn

    def multiply_self(target, g):
        for u in range(GROUP):
            k = g * GROUP + u
            x = plain[k]
            xt = plain_turn[k]
            put(target, u * nrow, x, x, xt)
            put(target, LANES + u * nrow, x, odd[k], odd_turn[k])
            put(target, 2 * LANES + u * nrow, x, halves_swapped(x), halves_swapped(xt))

    base = 3 * LANES

    bin_rows = lax.broadcasted_iota(jnp.int32, (nbins, LANES), 0)
    bin_rows = bin_rows.astype(jnp.float32).astype(jnp.bfloat16)
    one = jnp.ones((nbins, LANES), jnp.bfloat16)
    zero = jnp.zeros((nbins, LANES), jnp.bfloat16)

    def one_hot(row):
        return jnp.where(bin_rows == row.astype(jnp.bfloat16), one, zero)

    def select_self(part):
        first = part * half
        count = half - (part == 0)
        span(metas, first + (part == 0), count, send_m, recv_m.at[part]).wait_recv()
        spread = jnp.dot(
            metas[first : first + half, 0, :].astype(jnp.float32).astype(jnp.bfloat16),
            expand_ref[...],
            preferred_element_type=jnp.float32,
        )
        for u in range(half):
            cross_bins[first + u, 0:1, :] = spread[u : u + 1, 4 * LANES : 5 * LANES]
            cross_bins[first + u, 1:2, :] = spread[u : u + 1, 5 * LANES : 6 * LANES]
        self_bins = spread[:, : 4 * LANES]
        slot = lax.broadcasted_iota(jnp.int32, self_bins.shape, 0) % GROUP
        place = lax.broadcasted_iota(jnp.int32, self_bins.shape, 1) % LANES // nrow
        self_bins = jnp.where(slot == place, self_bins, 0.0)
        for v in range(half // GROUP):
            i = sequence.index(part * half // GROUP + v)
            row = jnp.sum(self_bins[v * GROUP : (v + 1) * GROUP], axis=0, keepdims=True)
            alone, ahead, back, over = [
                one_hot(row[:, h * LANES : (h + 1) * LANES]) for h in range(4)
            ]
            at = i * base
            for target, mixed in ((select_re, ahead + back), (select_im, ahead - back)):
                target[:, at : at + LANES] = alone
                target[:, at + LANES : at + 2 * LANES] = mixed
                target[:, at + 2 * LANES : at + 3 * LANES] = over

    def select_cross():
        for j in range(n // 2):
            ahead = one_hot(cross_bins[firsts[j], 0:1, :])
            back = one_hot(cross_bins[firsts[j] ^ mirror, 1:2, :])
            cross_re[:, j * LANES : (j + 1) * LANES] = ahead + back
            cross_im[:, j * LANES : (j + 1) * LANES] = ahead - back

    def product(left, right):
        return jnp.dot(left, right, preferred_element_type=jnp.float32)

    def multiply_cross(j):
        x = same[firsts[j]]
        q = firsts[j] ^ mirror
        at = j * LANES
        y, yt, z, zt = same[q], plain_turn[q], odd[q], odd_turn[q]
        put(cross_products, at, x, y, yt)
        put(cross_products, at + nrow, x, z, zt)
        put(cross_products, at + 2 * nrow, x, halves_swapped(y), halves_swapped(yt))
        put(cross_products, at + 3 * nrow, x, halves_swapped(z), halves_swapped(zt))

    def cross_sum(selector, first, last, columns):
        rows = slice(first * LANES, last * LANES)
        return product(selector[:, rows], cross_products[rows, columns])

    def self_sum(selector, i, columns):
        return product(selector[:, i * base : (i + 1) * base], products[i % 2, :, columns])

    real, imag = slice(0, nfreq), slice(nfreq, 2 * nfreq)
    def collect(i):
        g = sequence[i]
        here = range(max(g * GROUP, 1), (g + 1) * GROUP)
        span(plain, here[0], len(here), send_a, recv_a.at[g]).wait_recv()
        for k in range(g * GROUP, (g + 1) * GROUP):
            prepare(k)
        multiply_self(products.at[i % 2], g)

    collect(0)
    collect(1)
    select_self(0)
    total_re[...] = self_sum(select_re, 0, real) + self_sum(select_re, 1, real)
    total_im[...] = self_sum(select_im, 0, imag) + self_sum(select_im, 1, imag)
    select_self(1)
    select_cross()
    collect(2)
    for j in range(PLANE):
        multiply_cross(j)
    total_re[...] += self_sum(select_re, 2, real) + cross_sum(cross_re, 0, PLANE, real)
    total_im[...] += self_sum(select_im, 2, imag) + cross_sum(cross_im, 0, PLANE, imag)
    collect(3)
    for j in range(PLANE, 2 * PLANE):
        multiply_cross(j)
    last = ngroups - 1
    terms_re = (
        total_re[...]
        + self_sum(select_re, last, real)
        + cross_sum(cross_re, PLANE, 2 * PLANE, real)
    )
    terms_re = terms_re.reshape(n, nbins_dev, nfreq).astype(jnp.bfloat16)
    terms_im = (
        total_im[...]
        + self_sum(select_im, last, imag)
        + cross_sum(cross_im, PLANE, 2 * PLANE, imag)
    )
    terms_im = terms_im.reshape(n, nbins_dev, nfreq).astype(jnp.bfloat16)
    outgoing[:, :, real] = terms_re
    outgoing[:, :, imag] = terms_im

    for i in range(n - 1):
        target = i + (i + n - me) // n
        remote(outgoing.at[target], incoming.at[me], send_b, recv_b, target).start()
    incoming[me] = outgoing[me]
    copy_table.wait()
    copy_phase.wait()
    span(incoming, 0, n - 1, send_b, recv_b).wait_recv()

    arrived = incoming[...].astype(jnp.float32).reshape(nbins, 2 * nfreq).astype(jnp.bfloat16)
    stacked = jnp.concatenate([arrived[:, real], arrived[:, imag]], axis=0)
    zero_lag = LAGS // 2
    lane = lax.broadcasted_iota(jnp.int32, (nbins_dev, LANES), 1)
    backward = (LANES - lane) % LANES
    mirrored = []
    for a in range(lag_span() // LANES):
        both = slice(2 * a * LANES, 2 * (a + 1) * LANES)
        lags = product(stacked, table[:, both]).reshape(2, n, nbins_dev, 2 * LANES)
        cos, sin = phases[:, :, both][:, :, :LANES], phases[:, :, both][:, :, LANES:]
        even_part = jnp.sum(lags[0, :, :, :LANES] * cos - lags[0, :, :, LANES:] * sin, axis=0)
        odd_part = jnp.sum(lags[1, :, :, LANES:] * cos + lags[1, :, :, :LANES] * sin, axis=0)
        if a < zero_lag // LANES:
            out_ref[:, zero_lag + a * LANES : zero_lag + (a + 1) * LANES] = even_part - odd_part
        mirrored.append(even_part + odd_part)
    for a in range(zero_lag // LANES):
        high = mirrored[zero_lag // LANES - a]
        low = jnp.take_along_axis(mirrored[zero_lag // LANES - a - 1], backward, axis=1)
        out_ref[:, a * LANES : (a + 1) * LANES] = jnp.where(lane == 0, high, low)

    span(metas, 1, n - 1, send_m, recv_m.at[0]).wait_send()
    span(plain, 1, n - 1, send_a, recv_a.at[0]).wait_send()
    span(incoming, 0, n - 1, send_b, recv_b).wait_send()


def on_device_slices(spectra, valid, partner, pair_bin, pair_count):
    n = lax.axis_size("chan")
    nchan, nwin, _, nfreq_all = spectra.shape
    nfreq = nfreq_all // n
    nrow = nchan * nwin * 2
    nbins = n * BINS_DEV
    base = 3 * LANES
    deep = n // 2 * LANES
    scale = 1.0 / (math.sqrt(nfreq_all) * nwin * math.sqrt(PAIRS_DEV // BINS_DEV))
    hbm = pl.BlockSpec(memory_space=pltpu.HBM)
    vmem = pl.BlockSpec(memory_space=pltpu.VMEM)
    dma = pltpu.SemaphoreType.DMA
    bf16 = jnp.bfloat16
    return pl.pallas_call(
        functools.partial(kernel, (n, nchan, nwin, nfreq, BINS_DEV)),
        out_shape=pltpu.VMEM((BINS_DEV, LAGS), jnp.float32),
        in_specs=[hbm] * 8,
        out_specs=vmem,
        scratch_shapes=[
            pltpu.VMEM(spectra.shape, bf16),
            pltpu.SMEM(valid.shape, jnp.int32),
            pltpu.SMEM(partner.shape, jnp.int32),
            pltpu.SMEM(pair_bin.shape, jnp.int32),
            pltpu.SMEM(pair_count.shape, jnp.int32),
            pltpu.VMEM((LANES, 6 * LANES), bf16),
            pltpu.VMEM((1, LANES), jnp.int32),
            pltpu.VMEM((n, 1, LANES), jnp.int32),
            pltpu.VMEM((n, nrow, nfreq), bf16),
            pltpu.VMEM((n, nrow, nfreq), bf16),
            pltpu.VMEM((n, nrow, nfreq), bf16),
            pltpu.VMEM((n, nrow, nfreq), bf16),
            pltpu.VMEM((n, nrow, nfreq), bf16),
            pltpu.VMEM((n, nrow, nfreq), bf16),
            pltpu.VMEM((nfreq, 2 * lag_span()), bf16),
            pltpu.VMEM((n, 1, 2 * lag_span()), jnp.float32),
            pltpu.VMEM((n, 8, LANES), jnp.float32),
            pltpu.VMEM((nbins, n // GROUP * base), bf16),
            pltpu.VMEM((nbins, n // GROUP * base), bf16),
            pltpu.VMEM((nbins, deep), bf16),
            pltpu.VMEM((nbins, deep), bf16),
            pltpu.VMEM((2, base, 2 * nfreq), bf16),
            pltpu.VMEM((deep, 2 * nfreq), bf16),
            pltpu.VMEM((nbins, nfreq), jnp.float32),
            pltpu.VMEM((nbins, nfreq), jnp.float32),
            pltpu.VMEM((n, BINS_DEV, 2 * nfreq), bf16),
            pltpu.VMEM((n, BINS_DEV, 2 * nfreq), bf16),
            dma((8,)),
            dma,
            dma((n // GROUP,)),
            dma,
            dma((2,)),
            dma,
            dma,
            pltpu.SemaphoreType.REGULAR,
            pltpu.SemaphoreType.REGULAR,
        ],
        compiler_params=pltpu.CompilerParams(
            collective_id=0, has_side_effects=True, vmem_limit_bytes=60 * 1024 * 1024
        ),
    )(
        spectra,
        valid,
        partner,
        pair_bin,
        pair_count,
        jnp.asarray(expanders(nchan, nwin)),
        jnp.asarray(base_table(nfreq)),
        jnp.asarray(slice_phases(n, nfreq, scale)),
    )


def solution(mesh):
    in_specs = (
        P(("grp", "chan"), None, None, None),
        P(("grp", "chan"), None),
        P(),
        P(("grp", "chan")),
        P(("grp", "chan")),
    )
    out_specs = P(("grp", "chan"), None)
    nblocks = mesh.shape["chan"]
    whole_bands = F % (nblocks * BAND) == 0 and nblocks == GROUP * PLANE
    return jax.shard_map(
        on_device_slices if whole_bands else on_device_blocks,
        mesh=mesh,
        in_specs=in_specs,
        out_specs=out_specs,
        check_vma=False,
    )
```

```python
import functools
import math

import jax
import jax.numpy as jnp
import ml_dtypes
import numpy as np
from jax import lax
from jax.experimental import pallas as pl
from jax.experimental.pallas import tpu as pltpu
from jax.sharding import PartitionSpec as P

F = 4096
BAND = 128
LAGS = 1024
BINS_DEV = 8
PAIRS_DEV = 32
LANES = 128
GROUP = 4
PLANE = 4


def from_partner(block, axis, bit):
    count = lax.axis_size(axis)
    route = []
    for low in range(count):
        high = low | 1 << bit
        if high != low and high < count:
            route += [(low, high), (high, low)]
    return lax.ppermute(block, axis, route)


def whiten(spectra, valid):
    values = spectra.astype(jnp.float32)
    power = values[:, :, 0] * values[:, :, 0] + values[:, :, 1] * values[:, :, 1]
    nchan, nwin, nfreq = power.shape
    banded = jnp.mean(power.reshape(nchan, nwin, nfreq // BAND, BAND), axis=-1)
    amplitude = jnp.repeat(jnp.sqrt(banded + 1e-06), BAND, axis=-1)
    weights = valid.astype(jnp.float32)[:, :, None, None]
    return (values * weights / amplitude[:, :, None, :]).astype(jnp.bfloat16)


def lag_table():
    freqs = jnp.arange(F, dtype=jnp.int32)
    shifts = jnp.arange(LAGS, dtype=jnp.int32) - LAGS // 2
    phase = jnp.mod(freqs[:, None] * shifts[None, :], 2 * F)
    angle = phase.astype(jnp.float32) * (2.0 * math.pi / (2 * F))
    scale = 1.0 / math.sqrt(F)
    return jnp.concatenate([jnp.cos(angle) * scale, -jnp.sin(angle) * scale], axis=0).astype(
        jnp.bfloat16
    )


def cross_product(left_part, right_part):
    return jnp.einsum("awf,bwf->abf", left_part, right_part, preferred_element_type=jnp.float32)


def correlate(own_block, other_block, table):
    own_real = own_block[:, :, 0]
    own_imag = own_block[:, :, 1]
    oth_real = other_block[:, :, 0]
    oth_imag = other_block[:, :, 1]
    real_part = cross_product(own_real, oth_real) + cross_product(own_imag, oth_imag)
    imag_part = cross_product(own_imag, oth_real) - cross_product(own_real, oth_imag)
    nchan = own_block.shape[0]
    nwin = own_block.shape[1]
    spec = (jnp.concatenate([real_part, imag_part], axis=-1) * (1.0 / nwin)).reshape(
        nchan * nchan, -1
    )
    spec = spec.astype(jnp.bfloat16)
    return jnp.dot(spec, table, preferred_element_type=jnp.float32)


def select_sum(selector, corr_high, corr_low):
    return jnp.dot(selector, corr_high, preferred_element_type=jnp.float32) + jnp.dot(
        selector, corr_low, preferred_element_type=jnp.float32
    )


def on_device_blocks(spectra, valid, partner, pair_bin, pair_count):
    white = whiten(spectra, valid)
    nblocks = lax.axis_size("chan")
    round_mask = partner[0]
    paired = white
    for bit_index in range(nblocks.bit_length() - 1):
        swapped = from_partner(paired, "chan", bit_index)
        paired = jnp.where(round_mask >> bit_index & 1 == 1, swapped, paired)
    table = lag_table()
    self_corr = correlate(white, white, table)
    cross_corr = correlate(white, paired, table)
    corr = jnp.concatenate([self_corr, cross_corr], axis=0)
    corr_high = corr.astype(jnp.bfloat16)
    corr_low = (corr - corr_high.astype(jnp.float32)).astype(jnp.bfloat16)
    rows = jnp.arange(corr.shape[0], dtype=jnp.int32)
    live_rows = (rows < pair_count[0]) & (pair_bin >= 0)
    kept_bins = jnp.where(live_rows, pair_bin, -1)
    targets = lax.iota(jnp.int32, nblocks * BINS_DEV)
    selector = (kept_bins[None, :] == targets[:, None]).astype(jnp.bfloat16)
    terms = select_sum(selector, corr_high, corr_low).reshape(nblocks, BINS_DEV, -1)
    received = lax.all_to_all(terms, "chan", split_axis=0, concat_axis=0, tiled=True)
    summed = jnp.sum(received, axis=0)
    return summed * (1.0 / math.sqrt(PAIRS_DEV // BINS_DEV))


def lag_span():
    return LAGS // 2 + LANES


def interleaved(cos, sin):
    tiled = [part.reshape(part.shape[0], -1, 1, LANES) for part in (cos, sin)]
    return np.concatenate(tiled, axis=2).reshape(cos.shape[0], -1)


def base_table(nfreq):
    shifts = np.arange(lag_span())
    angle = np.mod(np.arange(nfreq)[:, None] * shifts[None, :], 2 * F) * (2.0 * math.pi / (2 * F))
    return interleaved(np.cos(angle), np.sin(angle)).astype(ml_dtypes.bfloat16)


def slice_phases(nslices, nfreq, scale):
    shifts = np.arange(lag_span())
    first = np.arange(nslices) * nfreq
    angle = np.mod(first[:, None] * shifts[None, :], 2 * F) * (2.0 * math.pi / (2 * F))
    both = interleaved(np.cos(angle), np.sin(angle)) * scale
    return both.astype(np.float32)[:, None, :]


def expanders(nchan, nwin):
    row = np.arange(LANES)
    per_chan = 2 * nwin
    chan = row // per_chan % nchan
    shift = row // (per_chan * nchan)
    npairs = nchan * nchan

    def pair(step):
        return chan * nchan + (chan + step) % nchan

    def reverse(step):
        return (chan + step) % nchan * nchan + chan

    lanes = (
        pair(0),
        pair(1),
        reverse(1),
        pair(2),
        npairs + pair(shift),
        npairs + reverse(shift),
    )
    return np.concatenate(
        [(np.arange(LANES)[:, None] == lane[None, :]) for lane in lanes], axis=1
    ).astype(ml_dtypes.bfloat16)


def swap_pairs(rows):
    size = rows.shape[-2]
    axis = rows.ndim - 2
    even = lax.broadcasted_iota(jnp.int32, rows.shape, axis) % 2 == 0
    return jnp.where(
        even, pltpu.roll(rows, size - 1, axis), pltpu.roll(rows, 1, axis)
    ), even


def halves_swapped(rows):
    half = rows.shape[0] // 2
    return jnp.concatenate([rows[half:], rows[:half]], axis=0)


def kernel(
    dims,
    spectra_hbm,
    valid_hbm,
    partner_hbm,
    bin_hbm,
    count_hbm,
    expand_hbm,
    table_hbm,
    phase_hbm,
    out_ref,
    own,
    valid_ref,
    partner_ref,
    bin_ref,
    count_ref,
    expand_ref,
    meta_ref,
    metas,
    white,
    plain,
    same,
    odd,
    plain_turn,
    odd_turn,
    table,
    phases,
    cross_bins,
    select_re,
    select_im,
    cross_re,
    cross_im,
    products,
    cross_products,
    total_re,
    total_im,
    outgoing,
    incoming,
    local_sems,
    send_a,
    recv_a,
    send_m,
    recv_m,
    send_b,
    recv_b,
    ready,
    token,
):
    n, nchan, nwin, nfreq, nbins_dev = dims
    nrow = nchan * nwin * 2
    nbins = n * nbins_dev
    npairs = nchan * nchan
    ngroups = n // GROUP
    half = n // 2
    me = lax.axis_index("chan")

    def peer(k):
        bits = range((n - 1).bit_length())
        return sum((me // 2**b + k // 2**b) % 2 * 2**b for b in bits)

    def remote(src, dst, send, recv, target):
        return pltpu.make_async_remote_copy(
            src_ref=src,
            dst_ref=dst,
            send_sem=send,
            recv_sem=recv,
            device_id={"chan": target},
            device_id_type=pl.DeviceIdType.MESH,
        )

    def span(buffer, first, count, send, recv):
        part = buffer.at[pl.ds(first, count)]
        return remote(part, part, send, recv, peer(1))

    copy_own = pltpu.make_async_copy(spectra_hbm, own, local_sems.at[0])
    copy_table = pltpu.make_async_copy(table_hbm, table, local_sems.at[1])
    copy_phase = pltpu.make_async_copy(phase_hbm, phases, local_sems.at[2])
    small = [
        pltpu.make_async_copy(src, dst, local_sems.at[3 + i])
        for i, (src, dst) in enumerate(
            (
                (valid_hbm, valid_ref),
                (bin_hbm, bin_ref),
                (count_hbm, count_ref),
                (partner_hbm, partner_ref),
                (expand_hbm, expand_ref),
            )
        )
    ]
    plane = me // PLANE
    is_last = plane == n // PLANE - 1
    barrier = pltpu.get_barrier_semaphore()

    def signal(sem, ks):
        for k in ks:
            pl.semaphore_signal(
                sem,
                inc=1,
                device_id={"chan": peer(k)},
                device_id_type=pl.DeviceIdType.MESH,
            )

    @pl.when(jnp.logical_not(is_last))
    def _():
        signal(barrier, range(n - 1, 0, -1))

    copy_own.start()
    for copy in small:
        copy.start()
    copy_table.start()
    copy_phase.start()
    for copy in small[:3]:
        copy.wait()

    lane = lax.broadcasted_iota(jnp.int32, meta_ref.shape, 1)
    bins = jnp.full(meta_ref.shape, -1, jnp.int32)
    for row in range(2 * npairs):
        bins = jnp.where(lane == row, bin_ref[row], bins)
    bins = jnp.where((lane < count_ref[0]) & (bins >= 0), bins, -1)
    meta_ref[...] = bins

    sub = lax.broadcasted_iota(jnp.int32, (nchan, 2 * nwin, LANES), 1) // 2
    chan = lax.broadcasted_iota(jnp.int32, (nchan, 2 * nwin, LANES), 0)
    usable = jnp.zeros((nchan, 2 * nwin, LANES), jnp.float32)
    for c in range(nchan):
        for w in range(nwin):
            usable = jnp.where(
                (chan == c) & (sub == w), valid_ref[c, w].astype(jnp.float32), usable
            )

    def whiten_slice(t):
        here = pl.ds(pl.multiple_of(t * nfreq, nfreq), nfreq)
        x = own[:, :, :, here].astype(jnp.float32)
        x = x.reshape(nchan, 2 * nwin, nfreq)
        swapped, _ = swap_pairs(x)
        power = x * x + swapped * swapped
        for b in range(nfreq // BAND):
            band = slice(b * BAND, (b + 1) * BAND)
            total = jnp.sum(power[:, :, band], axis=-1, keepdims=True)
            scale = lax.rsqrt(total * (1.0 / BAND) + 1e-06) * usable
            rows = (x[:, :, band] * scale).reshape(nrow, BAND)
            white[t, :, band] = rows.astype(jnp.bfloat16)

    def send_meta(k):
        remote(meta_ref, metas.at[k], send_m, recv_m.at[k // half], peer(k)).start()

    def send_white(k):
        remote(white.at[peer(k)], plain.at[k], send_a, recv_a.at[k // GROUP], peer(k)).start()

    def each(act, ks):
        for k in ks:
            act(k)

    near = [7, 6, 5, 4]
    middle = [11, 10, 9, 8]
    far = [15, 14, 13, 12]
    inside = [3, 2, 1]
    copy_own.wait()

    @pl.when(jnp.logical_not(is_last))
    def _():
        def step(i, carry):
            for u in range(4):
                whiten_slice(4 * i + u)
            return carry

        lax.fori_loop(0, n // 4, step, 0)
        pl.semaphore_wait(barrier, 3 * PLANE - 1)

    @pl.when(is_last)
    def _():
        pl.semaphore_wait(barrier, 3 * PLANE)
        signal(ready, far + middle + near)
        each(send_meta, far + middle + near)
        for k in far + middle + near:
            whiten_slice(peer(k))
            send_white(k)
        for k in [*inside, 0]:
            whiten_slice(peer(k))
        pl.semaphore_wait(token, 1)
        each(send_meta, inside)
        each(send_white, inside)

    @pl.when(plane == 2)
    def _():
        each(send_meta, far + middle + inside)
        each(send_white, middle + far)
        pl.semaphore_wait(ready, PLANE)
        signal(token, near[-1:])
        each(send_meta, near)
        each(send_white, near + inside)

    @pl.when(plane == 1)
    def _():
        each(send_meta, far + near + inside)
        each(send_white, far + near)
        pl.semaphore_wait(ready, PLANE)
        each(send_meta, middle)
        each(send_white, middle + inside)

    @pl.when(plane == 0)
    def _():
        each(send_meta, middle + near + inside)
        each(send_white, middle)
        pl.semaphore_wait(ready, PLANE)
        each(send_meta, far)
        each(send_white, far + near + inside)

    plain[0] = white[me]
    metas[0] = meta_ref[...]
    for copy in small[3:]:
        copy.wait()
    mirror = partner_ref[0]
    across = mirror // PLANE
    lead = jnp.where(across == 2, 1, 0)
    early, late = [], []
    for j in range(PLANE):
        inner = jnp.where(mirror == 2, j % 2, j % 2 * 2)
        early.append(jnp.where(across == 0, j // 2 * PLANE + inner, lead * PLANE + j))
        late.append(jnp.where(across == 0, (3 - j // 2) * PLANE + inner, 2 * PLANE + j))
    firsts = early + late
    sequence = [0, 1, 3, 2]

    def prepare(k):
        same[k] = plain[k]
        x = plain[k].astype(jnp.float32)
        swapped, even = swap_pairs(x)
        turn = jnp.where(even, -swapped, swapped)
        step = 2 * nwin
        odd[k] = jnp.concatenate([x[step:], x[:step]], axis=0).astype(jnp.bfloat16)
        plain_turn[k] = turn.astype(jnp.bfloat16)
        odd_turn[k] = jnp.concatenate([turn[step:], turn[:step]], axis=0).astype(jnp.bfloat16)

    def put(target, at, left, right, right_turn):
        target[pl.ds(at, nrow), 0:nfreq] = left * right
        target[pl.ds(at, nrow), nfreq : 2 * nfreq] = left * right_turn

    def multiply_self(target, g):
        for u in range(GROUP):
            k = g * GROUP + u
            x = plain[k]
            xt = plain_turn[k]
            put(target, u * nrow, x, x, xt)
            put(target, LANES + u * nrow, x, odd[k], odd_turn[k])
            put(target, 2 * LANES + u * nrow, x, halves_swapped(x), halves_swapped(xt))

    base = 3 * LANES

    bin_rows = lax.broadcasted_iota(jnp.int32, (nbins, LANES), 0)
    bin_rows = bin_rows.astype(jnp.float32).astype(jnp.bfloat16)
    one = jnp.ones((nbins, LANES), jnp.bfloat16)
    zero = jnp.zeros((nbins, LANES), jnp.bfloat16)

    def one_hot(row):
        return jnp.where(bin_rows == row.astype(jnp.bfloat16), one, zero)

    def select_self(part):
        first = part * half
        count = half - (part == 0)
        span(metas, first + (part == 0), count, send_m, recv_m.at[part]).wait_recv()
        spread = jnp.dot(
            metas[first : first + half, 0, :].astype(jnp.float32).astype(jnp.bfloat16),
            expand_ref[...],
            preferred_element_type=jnp.float32,
        )
        for u in range(half):
            cross_bins[first + u, 0:1, :] = spread[u : u + 1, 4 * LANES : 5 * LANES]
            cross_bins[first + u, 1:2, :] = spread[u : u + 1, 5 * LANES : 6 * LANES]
        self_bins = spread[:, : 4 * LANES]
        slot = lax.broadcasted_iota(jnp.int32, self_bins.shape, 0) % GROUP
        place = lax.broadcasted_iota(jnp.int32, self_bins.shape, 1) % LANES // nrow
        self_bins = jnp.where(slot == place, self_bins, 0.0)
        for v in range(half // GROUP):
            i = sequence.index(part * half // GROUP + v)
            row = jnp.sum(self_bins[v * GROUP : (v + 1) * GROUP], axis=0, keepdims=True)
            alone, ahead, back, over = [
                one_hot(row[:, h * LANES : (h + 1) * LANES]) for h in range(4)
            ]
            at = i * base
            for target, mixed in ((select_re, ahead + back), (select_im, ahead - back)):
                target[:, at : at + LANES] = alone
                target[:, at + LANES : at + 2 * LANES] = mixed
                target[:, at + 2 * LANES : at + 3 * LANES] = over

    def select_cross():
        for j in range(n // 2):
            ahead = one_hot(cross_bins[firsts[j], 0:1, :])
            back = one_hot(cross_bins[firsts[j] ^ mirror, 1:2, :])
            cross_re[:, j * LANES : (j + 1) * LANES] = ahead + back
            cross_im[:, j * LANES : (j + 1) * LANES] = ahead - back

    def product(left, right):
        return jnp.dot(left, right, preferred_element_type=jnp.float32)

    def multiply_cross(j):
        x = same[firsts[j]]
        q = firsts[j] ^ mirror
        at = j * LANES
        y, yt, z, zt = same[q], plain_turn[q], odd[q], odd_turn[q]
        put(cross_products, at, x, y, yt)
        put(cross_products, at + nrow, x, z, zt)
        put(cross_products, at + 2 * nrow, x, halves_swapped(y), halves_swapped(yt))
        put(cross_products, at + 3 * nrow, x, halves_swapped(z), halves_swapped(zt))

    def cross_sum(selector, first, last, columns):
        rows = slice(first * LANES, last * LANES)
        return product(selector[:, rows], cross_products[rows, columns])

    def self_sum(selector, i, columns):
        return product(selector[:, i * base : (i + 1) * base], products[i % 2, :, columns])

    real, imag = slice(0, nfreq), slice(nfreq, 2 * nfreq)
    def collect(i):
        g = sequence[i]
        here = range(max(g * GROUP, 1), (g + 1) * GROUP)
        span(plain, here[0], len(here), send_a, recv_a.at[g]).wait_recv()
        for k in range(g * GROUP, (g + 1) * GROUP):
            prepare(k)
        multiply_self(products.at[i % 2], g)

    collect(0)
    collect(1)
    select_self(0)
    total_re[...] = self_sum(select_re, 0, real) + self_sum(select_re, 1, real)
    total_im[...] = self_sum(select_im, 0, imag) + self_sum(select_im, 1, imag)
    select_self(1)
    select_cross()
    collect(2)
    for j in range(PLANE):
        multiply_cross(j)
    total_re[...] += self_sum(select_re, 2, real) + cross_sum(cross_re, 0, PLANE, real)
    total_im[...] += self_sum(select_im, 2, imag) + cross_sum(cross_im, 0, PLANE, imag)
    collect(3)
    for j in range(PLANE, 2 * PLANE):
        multiply_cross(j)
    last = ngroups - 1
    terms_re = (
        total_re[...]
        + self_sum(select_re, last, real)
        + cross_sum(cross_re, PLANE, 2 * PLANE, real)
    )
    terms_re = terms_re.reshape(n, nbins_dev, nfreq).astype(jnp.bfloat16)
    terms_im = (
        total_im[...]
        + self_sum(select_im, last, imag)
        + cross_sum(cross_im, PLANE, 2 * PLANE, imag)
    )
    terms_im = terms_im.reshape(n, nbins_dev, nfreq).astype(jnp.bfloat16)
    outgoing[:, :, real] = terms_re
    outgoing[:, :, imag] = terms_im

    for i in range(n - 1):
        target = i + (i + n - me) // n
        remote(outgoing.at[target], incoming.at[me], send_b, recv_b, target).start()
    incoming[me] = outgoing[me]
    copy_table.wait()
    copy_phase.wait()
    span(incoming, 0, n - 1, send_b, recv_b).wait_recv()

    arrived = incoming[...].astype(jnp.float32).reshape(nbins, 2 * nfreq).astype(jnp.bfloat16)
    stacked = jnp.concatenate([arrived[:, real], arrived[:, imag]], axis=0)
    zero_lag = LAGS // 2
    lane = lax.broadcasted_iota(jnp.int32, (nbins_dev, LANES), 1)
    backward = (LANES - lane) % LANES
    mirrored = []
    for a in range(lag_span() // LANES):
        both = slice(2 * a * LANES, 2 * (a + 1) * LANES)
        lags = product(stacked, table[:, both]).reshape(2, n, nbins_dev, 2 * LANES)
        cos, sin = phases[:, :, both][:, :, :LANES], phases[:, :, both][:, :, LANES:]
        even_part = jnp.sum(lags[0, :, :, :LANES] * cos - lags[0, :, :, LANES:] * sin, axis=0)
        odd_part = jnp.sum(lags[1, :, :, LANES:] * cos + lags[1, :, :, :LANES] * sin, axis=0)
        if a < zero_lag // LANES:
            out_ref[:, zero_lag + a * LANES : zero_lag + (a + 1) * LANES] = even_part - odd_part
        mirrored.append(even_part + odd_part)
    for a in range(zero_lag // LANES):
        high = mirrored[zero_lag // LANES - a]
        low = jnp.take_along_axis(mirrored[zero_lag // LANES - a - 1], backward, axis=1)
        out_ref[:, a * LANES : (a + 1) * LANES] = jnp.where(lane == 0, high, low)

    span(metas, 1, n - 1, send_m, recv_m.at[0]).wait_send()
    span(plain, 1, n - 1, send_a, recv_a.at[0]).wait_send()
    span(incoming, 0, n - 1, send_b, recv_b).wait_send()


def on_device_slices(spectra, valid, partner, pair_bin, pair_count):
    n = lax.axis_size("chan")
    nchan, nwin, _, nfreq_all = spectra.shape
    nfreq = nfreq_all // n
    nrow = nchan * nwin * 2
    nbins = n * BINS_DEV
    base = 3 * LANES
    deep = n // 2 * LANES
    scale = 1.0 / (math.sqrt(nfreq_all) * nwin * math.sqrt(PAIRS_DEV // BINS_DEV))
    hbm = pl.BlockSpec(memory_space=pltpu.HBM)
    vmem = pl.BlockSpec(memory_space=pltpu.VMEM)
    dma = pltpu.SemaphoreType.DMA
    bf16 = jnp.bfloat16
    return pl.pallas_call(
        functools.partial(kernel, (n, nchan, nwin, nfreq, BINS_DEV)),
        out_shape=pltpu.VMEM((BINS_DEV, LAGS), jnp.float32),
        in_specs=[hbm] * 8,
        out_specs=vmem,
        scratch_shapes=[
            pltpu.VMEM(spectra.shape, bf16),
            pltpu.SMEM(valid.shape, jnp.int32),
            pltpu.SMEM(partner.shape, jnp.int32),
            pltpu.SMEM(pair_bin.shape, jnp.int32),
            pltpu.SMEM(pair_count.shape, jnp.int32),
            pltpu.VMEM((LANES, 6 * LANES), bf16),
            pltpu.VMEM((1, LANES), jnp.int32),
            pltpu.VMEM((n, 1, LANES), jnp.int32),
            pltpu.VMEM((n, nrow, nfreq), bf16),
            pltpu.VMEM((n, nrow, nfreq), bf16),
            pltpu.VMEM((n, nrow, nfreq), bf16),
            pltpu.VMEM((n, nrow, nfreq), bf16),
            pltpu.VMEM((n, nrow, nfreq), bf16),
            pltpu.VMEM((n, nrow, nfreq), bf16),
            pltpu.VMEM((nfreq, 2 * lag_span()), bf16),
            pltpu.VMEM((n, 1, 2 * lag_span()), jnp.float32),
            pltpu.VMEM((n, 8, LANES), jnp.float32),
            pltpu.VMEM((nbins, n // GROUP * base), bf16),
            pltpu.VMEM((nbins, n // GROUP * base), bf16),
            pltpu.VMEM((nbins, deep), bf16),
            pltpu.VMEM((nbins, deep), bf16),
            pltpu.VMEM((2, base, 2 * nfreq), bf16),
            pltpu.VMEM((deep, 2 * nfreq), bf16),
            pltpu.VMEM((nbins, nfreq), jnp.float32),
            pltpu.VMEM((nbins, nfreq), jnp.float32),
            pltpu.VMEM((n, BINS_DEV, 2 * nfreq), bf16),
            pltpu.VMEM((n, BINS_DEV, 2 * nfreq), bf16),
            dma((8,)),
            dma,
            dma((n // GROUP,)),
            dma,
            dma((2,)),
            dma,
            dma,
            pltpu.SemaphoreType.REGULAR,
            pltpu.SemaphoreType.REGULAR,
        ],
        compiler_params=pltpu.CompilerParams(
            collective_id=0, has_side_effects=True, vmem_limit_bytes=60 * 1024 * 1024
        ),
    )(
        spectra,
        valid,
        partner,
        pair_bin,
        pair_count,
        jnp.asarray(expanders(nchan, nwin)),
        jnp.asarray(base_table(nfreq)),
        jnp.asarray(slice_phases(n, nfreq, scale)),
    )


def solution(mesh):
    in_specs = (
        P(("grp", "chan"), None, None, None),
        P(("grp", "chan"), None),
        P(),
        P(("grp", "chan")),
        P(("grp", "chan")),
    )
    out_specs = P(("grp", "chan"), None)
    nblocks = mesh.shape["chan"]
    whole_bands = F % (nblocks * BAND) == 0 and nblocks == GROUP * PLANE
    return jax.shard_map(
        on_device_slices if whole_bands else on_device_blocks,
        mesh=mesh,
        in_specs=in_specs,
        out_specs=out_specs,
        check_vma=False,
    )
```
